256 devices in a mesh: samp: 64 (over z, y, core), var: 4 (over x).
Axes of the slice: x: 4, y: 4, z: 8, core: 2. Of those that a mesh axis runs over, the one named last changes fastest.
Arguments:
- dosage: bfloat16 [16384, 40960], P('samp', 'var'), may hold values from 0 to 2
- centers: float32 [40960], replicated, may hold values from 0.4 to 1.34
- scales: float32 [40960], replicated, may hold values from 1.6 to 2.2
- phenotype: float32 [16384], P('samp'), may hold values from -6 to 6
- fold_ids: int32 [16384], P('samp'), may hold values from 0 to 3
- strong_blocks: int32 [32], replicated, may hold values from 0 to 319, as said below
- warm_start: float32 [4096, 32], replicated, may hold values from -4 to 4
- penalty: float32 [8], replicated, may hold values from 0.05 to 0.5
- step_size: float32 [32], replicated, may hold values from 0.2 to 0.6
Outputs:
- margin: float32 [40960], P('var')
- coefficients: float32 [4096, 32], P('var')
The draws below stay inside these ranges and needn't reach their ends.
Inputs may be any that keep to these rules, and one draw needn't show every extreme that they name: `strong_blocks`: 32 different block numbers.
All inputs are finite; a program needn't handle non-finite values.
Results may differ from the reference program's by a relative error of at most 0.0075.
Values may be sent and summed in bfloat16 or wider, within the bound.
No kernel may reach another device: no remote copies, remote signals or barrier semaphores. Data moves between devices by JAX's collectives and lax.ppermute only.
A program may use at most 64 MiB of HBM per device.

```python
import math
import jax
import jax.numpy as jnp
from jax import lax

BLOCK = 128
V = 40960
NS = 4096
LAMBDAS = 8
FOLDS = 4
ITERS = 3
SAMPLES = 16384
FITS = 32
VBLK = 320
NSB = 32
VB_DEV = 80


def allele_shape(key):
    lowest = jnp.log(jnp.float32(0.5))
    highest = jnp.log(jnp.float32(4.0))
    return jnp.exp(jax.random.uniform(jax.random.fold_in(key, 11), (V,), jnp.float32, lowest, highest))


def draw_dosage(key, part):
    power = allele_shape(key)
    noise = jax.random.uniform(jax.random.fold_in(key, 12), (SAMPLES, V), jnp.float32, 1e-06, 1.0)
    return (2.0 * noise ** power[None, :]).astype(jnp.bfloat16)


def draw_centers(key, part):
    power = allele_shape(key)
    return 2.0 / (1.0 + power)


def draw_scales(key, part):
    power = allele_shape(key)
    return (1.0 + power) * jnp.sqrt(1.0 + 2.0 * power) / (2.0 * power)


def draw_strong_blocks(key, part):
    favored = jax.random.randint(jax.random.fold_in(key, 21), (), 0, VBLK // VB_DEV)
    index = jnp.arange(VBLK, dtype=jnp.int32)
    scores = jax.random.randint(jax.random.fold_in(key, 22), (VBLK,), 0, 2 ** 20)
    scores = scores + jnp.where(index // VB_DEV == favored, 2 ** 18, 0).astype(jnp.int32)
    ends = (index == 0) | (index == VBLK - 1)
    scores = jnp.where(ends, 2 ** 21, scores).astype(jnp.int32)
    distinct = scores * VBLK + index
    return lax.top_k(distinct, NSB)[1].astype(jnp.int32)


def with_ends(drawn, own_key, least, high):
    shape = drawn.shape
    place = [jax.random.randint(jax.random.fold_in(own_key, axis), (), 0, shape[axis]) for axis in range(len(shape))]
    drawn = drawn.at[tuple(place)].set(least)
    longest = shape.index(max(shape))
    place[longest] = (place[longest] + 1) % shape[longest]
    return drawn.at[tuple(place)].set(high)


def level_of(key, shape, cuts, smallest, top_value):
    level, own = 1.0, jax.random.fold_in(key, 6)
    for axis_at, parts in cuts:
        steps = jnp.exp(jax.random.uniform(jax.random.fold_in(own, axis_at), (parts,), jnp.float32, smallest / len(cuts), top_value / len(cuts)))
        level = level * jnp.repeat(steps, shape[axis_at] // parts).reshape([-1 if axis == axis_at else 1 for axis in range(len(shape))])
    return level


def gaussian(rng, extent, width, bound, cuts=(), kind=jnp.bfloat16):
    gain = level_of(rng, extent, cuts, -0.22, 0.18) if cuts else 1.0
    result = jax.random.normal(rng, extent, jnp.float32) * width * gain
    return jnp.minimum(jnp.maximum(result, -bound), bound).astype(kind)


def setup_inputs(seed: int = 0) -> dict:
    key_list = jax.random.split(jax.random.key(seed), 10)
    dosage = draw_dosage(jax.random.fold_in(key_list[9], 71), 0)
    centers = draw_centers(jax.random.fold_in(key_list[9], 71), 0)
    scales = draw_scales(jax.random.fold_in(key_list[9], 71), 0)
    phenotype = gaussian(key_list[3], (SAMPLES,), 1.0, 6.0, ((0, 64),), jnp.float32)
    fold_ids = with_ends(jax.random.randint(key_list[4], (SAMPLES,), 0, FOLDS), jax.random.fold_in(key_list[4], 1), 0, FOLDS - 1).astype(jnp.int32)
    strong_blocks = draw_strong_blocks(jax.random.fold_in(key_list[9], 71), 0)
    warm_start = gaussian(key_list[6], (NS, FITS), 0.3, 4.0, (), jnp.float32)
    penalty = jnp.clip(jnp.exp(jax.random.uniform(key_list[7], (LAMBDAS,), jnp.float32, math.log(0.05), math.log(0.5))), 0.05, 0.5)
    step_size = jnp.clip(jax.random.uniform(key_list[8], (FITS,), jnp.float32, 0.2, 0.6), 0.2, 0.6)
    return {"dosage": dosage, "centers": centers, "scales": scales, "phenotype": phenotype, "fold_ids": fold_ids, "strong_blocks": strong_blocks, "warm_start": warm_start, "penalty": penalty, "step_size": step_size}


exact_mode = lax.Precision.HIGHEST

def reference(dosage, centers, scales, phenotype, fold_ids, strong_blocks, warm_start, penalty, step_size):
    fit_folds = jnp.arange(LAMBDAS * FOLDS, dtype=jnp.int32) % FOLDS
    weights = (fold_ids[:, None] != fit_folds[None, :]).astype(jnp.float32)
    counts = lax.optimization_barrier(jnp.sum(weights, axis=0))
    fit_penalty = jnp.repeat(penalty, FOLDS)
    threshold = step_size * fit_penalty
    columns = (strong_blocks[:, None] * BLOCK + jnp.arange(BLOCK, dtype=jnp.int32)[None, :]).reshape(NS).astype(jnp.int32)
    strong = jnp.take(dosage, columns, axis=1).astype(jnp.float32)
    strong_centers = centers[columns]
    strong_scales = scales[columns]

    def residual_of(coef):
        scaled = (strong_scales[:, None] * coef).astype(jnp.bfloat16).astype(jnp.float32)
        fitted = jnp.dot(strong, scaled, precision=exact_mode)
        fitted = fitted - jnp.dot(strong_centers * strong_scales, coef, precision=exact_mode)[None, :]
        return (weights * (phenotype[:, None] - fitted)).astype(jnp.bfloat16)

    def cross_of(matrix, rounded):
        return jnp.dot(matrix.astype(jnp.float32).T, rounded.astype(jnp.float32), precision=exact_mode)
    rounded = residual_of(warm_start)
    column_sums = lax.optimization_barrier(jnp.sum(rounded.astype(jnp.float32), axis=0))
    slab = V // 8
    pieces = []
    for index in range(8):
        pieces.append(cross_of(dosage[:, index * slab:(index + 1) * slab], rounded))
    full_cross = jnp.concatenate(pieces, axis=0)
    kkt = scales[:, None] * (full_cross - centers[:, None] * column_sums[None, :]) / counts[None, :]
    margin = lax.optimization_barrier(jnp.max(jnp.abs(kkt) / fit_penalty[None, :], axis=1))
    momentum = 1.0
    point = warm_start
    previous = warm_start
    for sweep in range(ITERS):
        if sweep > 0:
            rounded = residual_of(point)
            column_sums = lax.optimization_barrier(jnp.sum(rounded.astype(jnp.float32), axis=0))
        gradient = strong_scales[:, None] * (cross_of(strong, rounded) - strong_centers[:, None] * column_sums[None, :]) / counts[None, :]
        moved = point + step_size[None, :] * gradient
        current = moved - jnp.clip(moved, -threshold[None, :], threshold[None, :])
        following = (1.0 + math.sqrt(1.0 + 4.0 * momentum * momentum)) / 2.0
        point = current + (momentum - 1.0) / following * (current - previous)
        previous = current
        momentum = following
    return (margin, previous)
```

```python
import functools
import math

import jax
import jax.numpy as jnp
from jax import lax
from jax.experimental import pallas as pl
from jax.experimental.pallas import tpu as pltpu
from jax.sharding import Mesh
from jax.sharding import PartitionSpec as P

BLOCK = 128
SLOTS = 32
NS = SLOTS * BLOCK
LAMBDAS = 8
FOLDS = 4
FITS = LAMBDAS * FOLDS
HALF = FITS // 2
ITERS = 3
PLANE = ("z", "y")
PARTS = 32
MBLK = 3

f32 = jnp.float32
bf16 = jnp.bfloat16
exact_mode = lax.Precision.HIGHEST


def pick_kernel(width, index_ref, source_ref, out_ref, sem):
    def start(slot, carry):
        pltpu.make_async_copy(
            source_ref.at[:, pl.ds(pl.multiple_of(index_ref[slot] * BLOCK, BLOCK), BLOCK)],
            out_ref.at[:, pl.ds(pl.multiple_of(slot * BLOCK, BLOCK), BLOCK)],
            sem,
        ).start()
        return carry

    lax.fori_loop(0, SLOTS, start, 0)
    pltpu.make_async_copy(source_ref.at[:, pl.ds(0, NS)], out_ref, sem).wait()


def pick_blocks(dosage, index):
    rows, width = dosage.shape
    return pl.pallas_call(
        functools.partial(pick_kernel, width),
        grid_spec=pltpu.PrefetchScalarGridSpec(
            num_scalar_prefetch=1,
            grid=(1,),
            in_specs=[pl.BlockSpec(memory_space=pl.ANY)],
            out_specs=pl.BlockSpec((rows, NS), lambda i, s: (0, 0)),
            scratch_shapes=[pltpu.SemaphoreType.DMA],
        ),
        out_shape=jax.ShapeDtypeStruct((rows, NS), bf16),
        name="pick_blocks",
    )(index, dosage)


def spread(payload, axis, count):
    return lax.all_to_all(
        jnp.broadcast_to(payload[None], (count,) + payload.shape), axis, 0, 0, tiled=True
    )


def swap(value):
    return lax.ppermute(value, "core", [(0, 1), (1, 0)])


def pieces(value):
    high = value.astype(bf16)
    rest = value - high.astype(f32)
    middle = rest.astype(bf16)
    low = (rest - middle.astype(f32)).astype(bf16)
    return [high, middle, low]


def lanes(wide):
    return wide.reshape(wide.shape[0], -1, BLOCK).transpose(1, 0, 2)


def shards(
    dosage, centers, scales, phenotype, fold_ids, strong_blocks, warm_start, penalty, step_size
):
    rows, local_width = dosage.shape
    local_blocks = local_width // BLOCK
    core = lax.axis_index("core")
    place = lax.axis_index("x")
    slot = lax.axis_index(PLANE)

    relative = strong_blocks - place * local_blocks
    owned = (relative >= 0) & (relative < local_blocks)
    own_mask = owned.astype(f32)
    mine = pick_blocks(dosage, jnp.clip(relative, 0, local_blocks - 1).astype(jnp.int32))
    other = swap(mine)

    center_rows = centers.reshape(-1, BLOCK)
    scale_rows = scales.reshape(-1, BLOCK)
    strong_centers = center_rows[strong_blocks]
    strong_scales = scale_rows[strong_blocks]
    flat_centers = strong_centers.reshape(1, NS)
    samples = jnp.stack([fold_ids.astype(f32), phenotype])
    samples_other = swap(samples)

    fit_folds = (jnp.arange(FITS, dtype=jnp.int32) % FOLDS).astype(f32)
    weights = (samples[:1] != fit_folds[:, None]).astype(f32)
    warm = warm_start.T
    coef_mask = jnp.repeat(own_mask, BLOCK)[None, :]
    flat_scales = strong_scales.reshape(1, NS)
    scaled = ((flat_scales * warm) * coef_mask).astype(bf16)
    shift = jnp.sum(warm * (flat_centers * flat_scales * coef_mask), axis=1, keepdims=True)
    dims = (((1,), (1,)), ((), ()))
    fit_part = lax.dot_general(scaled, mine, dims, preferred_element_type=f32) - shift
    fitted = jnp.sum(spread(fit_part.astype(bf16), "x", 4).astype(f32), axis=0)
    residual = (weights * (samples[1:] - fitted)).astype(bf16)
    column_sums = jnp.sum(residual.astype(f32), axis=1, keepdims=True)

    local_centers = lax.dynamic_slice_in_dim(centers, place * local_width, local_width, 0)
    local_scales = lax.dynamic_slice_in_dim(
        scale_rows, place * local_blocks, local_blocks, 0
    )
    cross = jnp.dot(residual, dosage, preferred_element_type=f32) - (
        local_centers[None, :] * column_sums
    )
    cross_strong = jnp.dot(residual, mine, preferred_element_type=f32) - (
        flat_centers * column_sums
    )
    both = jnp.concatenate([cross, cross_strong], axis=1)
    keep = lax.dynamic_slice_in_dim(both, core * HALF, HALF, 0)
    give = lax.dynamic_slice_in_dim(both, (1 - core) * HALF, HALF, 0)
    tally = jnp.sum(weights[:FOLDS], axis=1)
    tally_row = jnp.zeros((1, BLOCK), f32).at[0, :FOLDS].set(tally)
    summed = (keep + swap(give.astype(bf16)).astype(f32)).astype(bf16)
    tiles = lanes(summed)
    padded = jnp.concatenate(
        [tiles[:local_blocks], jnp.zeros((PARTS * MBLK - local_blocks, HALF, BLOCK), bf16)], axis=0
    ).reshape(PARTS, MBLK * HALF, BLOCK)
    tally_other = jnp.sum(
        (samples_other[:1] != fit_folds[:FOLDS, None]).astype(f32), axis=1
    )
    tally_rows = jnp.zeros((8, BLOCK), f32)
    tally_rows = tally_rows.at[0, :FOLDS].set(tally).at[1, :FOLDS].set(tally_other)
    message = jnp.concatenate(
        [
            padded,
            tiles[local_blocks:],
            jnp.broadcast_to(tally_rows.astype(bf16)[None], (PARTS, 8, BLOCK)),
        ],
        axis=1,
    )
    first = jnp.sum(lax.all_to_all(message, PLANE, 0, 0, tiled=True).astype(f32), axis=0)
    edge = MBLK * HALF
    totals = first[edge + HALF] + first[edge + HALF + 1]
    counts = jnp.tile(totals[:FOLDS], HALF // FOLDS)[:, None]

    fit_penalty = jnp.repeat(penalty, FOLDS)
    half_penalty = lax.dynamic_slice_in_dim(fit_penalty, core * HALF, HALF, 0)[:, None]
    step = lax.dynamic_slice_in_dim(step_size, core * HALF, HALF, 0)[:, None]
    threshold = step * half_penalty

    margin_scales = jnp.concatenate(
        [local_scales, jnp.zeros((PARTS * MBLK - local_blocks, BLOCK), f32)], axis=0
    )
    margin_scales = lax.dynamic_slice_in_dim(margin_scales, slot * MBLK, MBLK, 0)
    kkt = margin_scales[:, None, :] * first[:edge].reshape(MBLK, HALF, BLOCK) / counts[None]
    peak = jnp.max(jnp.abs(kkt) / half_penalty[None], axis=1)

    slot_scale = lax.dynamic_slice_in_dim(strong_scales, slot, 1, 0)
    slot_center = lax.dynamic_slice_in_dim(strong_centers, slot, 1, 0)
    slot_mask = lax.dynamic_slice_in_dim(own_mask, slot, 1, 0)[:, None]
    point = lax.dynamic_slice(warm, (core * HALF, slot * BLOCK), (HALF, BLOCK))
    previous = point
    gradient = first[edge : edge + HALF]
    near = jnp.concatenate([samples, samples_other], axis=1)
    half_weights = (near[:1] != fit_folds[:HALF, None]).astype(f32)
    momentum = 1.0
    margin = None
    for sweep in range(ITERS):
        if sweep > 0:
            coef = (slot_scale * point * slot_mask).astype(bf16)
            shift = jnp.sum(slot_center * slot_scale * slot_mask * point, axis=1)
            shift_row = jnp.concatenate(pieces(shift) + [jnp.zeros((BLOCK - 3 * HALF,), bf16)])
            parts = [coef, shift_row[None]]
            if sweep == 1:
                parts += pieces(peak)
            used = sum(part.shape[0] for part in parts)
            parts.append(jnp.zeros((-used % 8, BLOCK), bf16))
            got = spread(jnp.concatenate(parts, axis=0), PLANE, PARTS)
            if sweep == 1:
                peaks = got[:, HALF + 1 : HALF + 1 + 3 * MBLK].astype(f32)
                peaks = jnp.sum(peaks.reshape(PARTS, 3, MBLK, BLOCK), axis=1)
                peaks = peaks.reshape(PARTS * MBLK * BLOCK)[:local_width]
                margin = jnp.maximum(peaks, swap(peaks))
            scaled = got[:, :HALF].transpose(1, 0, 2).reshape(HALF, NS)
            shift = jnp.sum(got[:, HALF].astype(f32), axis=0)
            shift = jnp.sum(shift[: 3 * HALF].reshape(3, HALF), axis=0)[:, None]
            fit_part = jnp.concatenate(
                [
                    lax.dot_general(scaled, mine, dims, preferred_element_type=f32),
                    lax.dot_general(scaled, other, dims, preferred_element_type=f32),
                ],
                axis=1,
            )
            fit_part = (fit_part - shift).astype(bf16)
            fitted = jnp.sum(spread(fit_part, "x", 4).astype(f32), axis=0)
            residual = (half_weights * (near[1:] - fitted)).astype(bf16)
            column_sums = jnp.sum(residual.astype(f32), axis=1, keepdims=True)
            cross = jnp.dot(residual[:, :rows], mine, preferred_element_type=f32) + jnp.dot(
                residual[:, rows:], other, preferred_element_type=f32
            )
            cross = (cross - flat_centers * column_sums).astype(bf16)
            gradient = jnp.sum(
                lax.all_to_all(lanes(cross), PLANE, 0, 0, tiled=True).astype(f32), axis=0
            )
        moved = point + step * (slot_scale * gradient / counts)
        current = moved - jnp.clip(moved, -threshold, threshold)
        following = (1.0 + math.sqrt(1.0 + 4.0 * momentum * momentum)) / 2.0
        point = current + (momentum - 1.0) / following * (current - previous)
        previous = current
        momentum = following

    gathered = spread(previous * slot_mask, ("core", "x"), 8)
    whole = jnp.sum(gathered.reshape(2, 4, HALF, BLOCK), axis=1).reshape(FITS, BLOCK)
    everyone = spread(whole, PLANE, PARTS)
    share = SLOTS // 4
    out = lax.dynamic_slice_in_dim(everyone, place * share, share, 0)
    coefficients = out.transpose(0, 2, 1).reshape(share * BLOCK, FITS)
    return (margin, coefficients)


def solution(mesh):
    cube = Mesh(mesh.devices.reshape(8, 4, 2, 4), ("z", "y", "core", "x"))
    samp = ("z", "y", "core")
    return jax.shard_map(
        shards,
        mesh=cube,
        in_specs=(P(samp, "x"), P(), P(), P(samp), P(samp), P(), P(), P(), P()),
        out_specs=(P("x"), P("x", None)),
        check_vma=False,
    )
```

```python
import functools
import math

import jax
import jax.numpy as jnp
from jax import lax
from jax.experimental import pallas as pl
from jax.experimental.pallas import tpu as pltpu
from jax.sharding import Mesh
from jax.sharding import PartitionSpec as P

BLOCK = 128
SLOTS = 32
NS = SLOTS * BLOCK
LAMBDAS = 8
FOLDS = 4
FITS = LAMBDAS * FOLDS
HALF = FITS // 2
OWN = 4
SHARE = NS // 4
ITERS = 3
PLANE = ("z", "y")
PARTS = 32
MBLK = 3

f32 = jnp.float32
bf16 = jnp.bfloat16
exact_mode = lax.Precision.HIGHEST


def pick_kernel(width, index_ref, source_ref, out_ref, sem):
    def start(slot, carry):
        pltpu.make_async_copy(
            source_ref.at[:, pl.ds(pl.multiple_of(index_ref[slot] * BLOCK, BLOCK), BLOCK)],
            out_ref.at[:, pl.ds(pl.multiple_of(slot * BLOCK, BLOCK), BLOCK)],
            sem,
        ).start()
        return carry

    lax.fori_loop(0, SLOTS, start, 0)
    pltpu.make_async_copy(source_ref.at[:, pl.ds(0, NS)], out_ref, sem).wait()


def pick_blocks(dosage, index):
    rows, width = dosage.shape
    return pl.pallas_call(
        functools.partial(pick_kernel, width),
        grid_spec=pltpu.PrefetchScalarGridSpec(
            num_scalar_prefetch=1,
            grid=(1,),
            in_specs=[pl.BlockSpec(memory_space=pl.ANY)],
            out_specs=pl.BlockSpec((rows, NS), lambda i, s: (0, 0)),
            scratch_shapes=[pltpu.SemaphoreType.DMA],
        ),
        out_shape=jax.ShapeDtypeStruct((rows, NS), bf16),
        name="pick_blocks",
    )(index, dosage)


def spread(payload, axis, count):
    return lax.all_to_all(
        jnp.broadcast_to(payload[None], (count,) + payload.shape), axis, 0, 0, tiled=True
    )


def swap(value):
    return lax.ppermute(value, "core", [(0, 1), (1, 0)])


def onward(value):
    return lax.ppermute(value, "x", [(i, (i + 1) % 4) for i in range(4)])


def backward(value):
    return lax.ppermute(value, "x", [(i, (i + 3) % 4) for i in range(4)])


def turned(value, count, axis):
    twice = jnp.concatenate([value, value], axis=axis)
    return lax.dynamic_slice_in_dim(twice, count, value.shape[axis], axis)


def pieces(value):
    high = value.astype(bf16)
    rest = value - high.astype(f32)
    middle = rest.astype(bf16)
    low = (rest - middle.astype(f32)).astype(bf16)
    return [high, middle, low]


def lanes(wide):
    return wide.reshape(wide.shape[0], -1, BLOCK).transpose(1, 0, 2)


def shards(
    dosage, centers, scales, phenotype, fold_ids, strong_blocks, warm_start, penalty, step_size
):
    rows, local_width = dosage.shape
    part = rows // 2
    local_blocks = local_width // BLOCK
    core = lax.axis_index("core")
    place = lax.axis_index("x")
    slot = lax.axis_index(PLANE)

    relative = strong_blocks - place * local_blocks
    owned = (relative >= 0) & (relative < local_blocks)
    own_mask = owned.astype(f32)
    mine = pick_blocks(dosage, jnp.clip(relative, 0, local_blocks - 1).astype(jnp.int32))

    def chunk(ahead):
        return lax.dynamic_slice_in_dim(mine, (place + ahead) % 4 * SHARE, SHARE, 1)

    far = chunk(2)
    from_left = onward(jnp.concatenate([chunk(1), far[:part]], axis=0))
    from_right = backward(jnp.concatenate([chunk(3), far[part:]], axis=0))

    center_rows = centers.reshape(-1, BLOCK)
    scale_rows = scales.reshape(-1, BLOCK)
    strong_centers = center_rows[strong_blocks]
    strong_scales = scale_rows[strong_blocks]
    flat_centers = strong_centers.reshape(1, NS)
    samples = jnp.stack([fold_ids.astype(f32), phenotype])
    samples_other = swap(samples)

    fit_folds = (jnp.arange(FITS, dtype=jnp.int32) % FOLDS).astype(f32)
    weights = (samples[:1] != fit_folds[:, None]).astype(f32)
    warm = warm_start.T
    coef_mask = jnp.repeat(own_mask, BLOCK)[None, :]
    flat_scales = strong_scales.reshape(1, NS)
    scaled = ((flat_scales * warm) * coef_mask).astype(bf16)
    shift = jnp.sum(warm * (flat_centers * flat_scales * coef_mask), axis=1, keepdims=True)
    dims = (((1,), (1,)), ((), ()))
    fit_part = lax.dot_general(scaled, mine, dims, preferred_element_type=f32) - shift
    fitted = jnp.sum(spread(fit_part.astype(bf16), "x", 4).astype(f32), axis=0)
    residual = (weights * (samples[1:] - fitted)).astype(bf16)
    column_sums = jnp.sum(residual.astype(f32), axis=1, keepdims=True)

    local_centers = lax.dynamic_slice_in_dim(centers, place * local_width, local_width, 0)
    local_scales = lax.dynamic_slice_in_dim(scale_rows, place * local_blocks, local_blocks, 0)
    cross = jnp.dot(residual, dosage, preferred_element_type=f32) - (
        local_centers[None, :] * column_sums
    )
    cross_strong = jnp.dot(residual, mine, preferred_element_type=f32) - (
        flat_centers * column_sums
    )
    both = jnp.concatenate([cross, cross_strong], axis=1)
    keep = lax.dynamic_slice_in_dim(both, core * HALF, HALF, 0)
    give = lax.dynamic_slice_in_dim(both, (1 - core) * HALF, HALF, 0)
    summed = (keep + swap(give.astype(bf16)).astype(f32)).astype(bf16)
    tiles = lanes(summed)
    padded = jnp.concatenate(
        [tiles[:local_blocks], jnp.zeros((PARTS * MBLK - local_blocks, HALF, BLOCK), bf16)], axis=0
    ).reshape(PARTS, MBLK * HALF, BLOCK)
    near = jnp.concatenate([samples, samples_other], axis=1)
    half_weights = (near[:1] != fit_folds[:FOLDS, None]).astype(f32)
    tally_rows = jnp.zeros((8, BLOCK), f32)
    tally_rows = tally_rows.at[0, :FOLDS].set(jnp.sum(half_weights[:, :rows], axis=1))
    tally_rows = tally_rows.at[1, :FOLDS].set(jnp.sum(half_weights[:, rows:], axis=1))
    message = jnp.concatenate(
        [
            padded,
            tiles[local_blocks:],
            jnp.broadcast_to(tally_rows.astype(bf16)[None], (PARTS, 8, BLOCK)),
        ],
        axis=1,
    )
    message, from_left, from_right = lax.optimization_barrier((message, from_left, from_right))
    via_left = onward(from_left[rows:])
    via_right = backward(from_right[rows:])
    first = jnp.sum(lax.all_to_all(message, PLANE, 0, 0, tiled=True).astype(f32), axis=0)
    edge = MBLK * HALF
    totals = first[edge + HALF] + first[edge + HALF + 1]
    counts = totals[:FOLDS, None]

    def mine_of(values, start, size):
        return lax.dynamic_slice_in_dim(values, start, size, 0)[:, None]

    fit_penalty = jnp.repeat(penalty, FOLDS)
    half_penalty = mine_of(fit_penalty, core * HALF, HALF)
    step = mine_of(step_size, core * HALF, HALF)
    half_counts = jnp.tile(counts, (HALF // FOLDS, 1))

    margin_scales = jnp.concatenate(
        [local_scales, jnp.zeros((PARTS * MBLK - local_blocks, BLOCK), f32)], axis=0
    )
    margin_scales = lax.dynamic_slice_in_dim(margin_scales, slot * MBLK, MBLK, 0)
    kkt = margin_scales[:, None, :] * first[:edge].reshape(MBLK, HALF, BLOCK) / half_counts[None]
    peak = jnp.max(jnp.abs(kkt) / half_penalty[None], axis=1)

    slot_scale = lax.dynamic_slice_in_dim(strong_scales, slot, 1, 0)
    slot_mask = lax.dynamic_slice_in_dim(own_mask, slot, 1, 0)[:, None]
    point = lax.dynamic_slice(warm, (core * HALF, slot * BLOCK), (HALF, BLOCK))
    moved = point + step * (slot_scale * first[edge : edge + HALF] / half_counts)
    threshold = step * half_penalty
    current = (moved - jnp.clip(moved, -threshold, threshold)) * slot_mask

    current, via_left, via_right = lax.optimization_barrier((current, via_left, via_right))
    owner = jnp.repeat(strong_blocks // local_blocks, BLOCK)
    owner = lax.dynamic_slice_in_dim(owner, place * SHARE, SHARE, 0)[None, :]
    share = jnp.where(owner == (place + 3) % 4, from_left[:rows], chunk(0))
    share = jnp.where(owner == (place + 1) % 4, from_right[:rows], share)
    share = jnp.where(
        owner == (place + 2) % 4, jnp.concatenate([via_left, via_right], axis=0), share
    )
    share_left = onward(share)
    share_right = backward(share)
    share_other = swap(share)
    mixed = lax.all_to_all(current.reshape(4, OWN, BLOCK), "x", 0, 0, tiled=True)
    parts = pieces(jnp.sum(mixed, axis=0)) + pieces(peak)
    used = sum(piece.shape[0] for piece in parts)
    parts.append(jnp.zeros((-used % 8, BLOCK), bf16))
    payload = jnp.concatenate(parts, axis=0)
    payload, share_left, share_right, share_other = lax.optimization_barrier(
        (payload, share_left, share_right, share_other)
    )
    share_far = [onward(share_left[:part]), backward(share_right[part:])]
    left_other, right_other = swap(share_left), swap(share_right)
    got = spread(payload, PLANE, PARTS)
    peaks = got[:, 3 * OWN : 3 * OWN + 3 * MBLK].astype(f32)
    peaks = jnp.sum(peaks.reshape(PARTS, 3, MBLK, BLOCK), axis=1)
    peaks = peaks.reshape(PARTS * MBLK * BLOCK)[:local_width]
    margin = jnp.maximum(peaks, swap(peaks))
    current = jnp.sum(got[:, : 3 * OWN].astype(f32).reshape(PARTS, 3, OWN, BLOCK), axis=1)
    ahead = place * (SLOTS // 4)
    current = turned(current, ahead, 0).transpose(1, 0, 2).reshape(OWN, NS)
    wide_scale = turned(strong_scales, ahead, 0).reshape(1, NS)
    wide_center = turned(strong_centers, ahead, 0).reshape(1, NS)
    far_other = [swap(piece) for piece in share_far]
    strong = jnp.concatenate(
        [
            jnp.concatenate([share, share_right, jnp.concatenate(share_far, axis=0), share_left], axis=1),
            jnp.concatenate(
                [share_other, right_other, jnp.concatenate(far_other, axis=0), left_other], axis=1
            ),
        ],
        axis=0,
    )

    first_fit = core * HALF + place * OWN
    step = mine_of(step_size, first_fit, OWN)
    threshold = step * mine_of(fit_penalty, first_fit, OWN)
    point = current
    previous = current
    momentum = (1.0 + math.sqrt(5.0)) / 2.0
    for sweep in range(1, ITERS):
        scaled = (wide_scale * point).astype(bf16)
        shift = jnp.sum(wide_center * wide_scale * point, axis=1, keepdims=True)
        fitted = lax.dot_general(scaled, strong, dims, preferred_element_type=f32) - shift
        residual = (half_weights * (near[1:] - fitted)).astype(bf16)
        column_sums = jnp.sum(residual.astype(f32), axis=1, keepdims=True)
        cross = jnp.dot(residual, strong, preferred_element_type=f32) - wide_center * column_sums
        cross = jnp.sum(spread(cross.astype(bf16), "y", 4).astype(f32), axis=0)
        cross = jnp.sum(spread(cross.astype(bf16), "z", 8).astype(f32), axis=0)
        moved = point + step * (wide_scale * cross / counts)
        current = moved - jnp.clip(moved, -threshold, threshold)
        following = (1.0 + math.sqrt(1.0 + 4.0 * momentum * momentum)) / 2.0
        point = current + (momentum - 1.0) / following * (current - previous)
        previous = current
        momentum = following

    leaving = previous.reshape(OWN, 4, SHARE).transpose(1, 0, 2)
    leaving = turned(leaving, (4 - place) % 4, 0)
    landed = lax.all_to_all(
        jnp.concatenate([leaving, leaving], axis=0), ("core", "x"), 0, 0, tiled=True
    )
    coefficients = landed.reshape(FITS, SHARE).T
    return (margin, coefficients)


def solution(mesh):
    cube = Mesh(mesh.devices.reshape(8, 4, 2, 4), ("z", "y", "core", "x"))
    samp = ("z", "y", "core")
    return jax.shard_map(
        shards,
        mesh=cube,
        in_specs=(P(samp, "x"), P(), P(), P(samp), P(samp), P(), P(), P(), P()),
        out_specs=(P("x"), P("x", None)),
        check_vma=False,
    )
```

```python
import functools
import math

import jax
import jax.numpy as jnp
from jax import lax
from jax.experimental import pallas as pl
from jax.experimental.pallas import tpu as pltpu
from jax.sharding import Mesh
from jax.sharding import PartitionSpec as P

BLOCK = 128
SLOTS = 32
NS = SLOTS * BLOCK
LAMBDAS = 8
FOLDS = 4
FITS = LAMBDAS * FOLDS
HALF = FITS // 2
OWN = 4
SHARE = NS // 4
EACH = SHARE // BLOCK
ITERS = 3
PLANE = ("z", "y")
PARTS = 32
MBLK = 3
ROWS = 256
PART = ROWS // 2
PEAK = MBLK * BLOCK

f32 = jnp.float32
bf16 = jnp.bfloat16
LAST = (((1,), (1,)), ((), ()))
WHOLE = pl.BlockSpec(memory_space=pltpu.VMEM)


def pick_kernel(
    index_ref, source_ref, scaled_ref, shift_ref, own, right, far_a, far_b, left, fit_ref, sem
):
    moves = (
        (own, 0, 0, ROWS),
        (right, 1, 0, ROWS),
        (far_a, 2, 0, PART),
        (far_b, 2, PART, PART),
        (left, 3, 0, ROWS),
    )
    copies = []
    for target, turn, first, height in moves:
        for i in range(EACH):
            block = index_ref[turn * EACH + i]
            copies.append(
                pltpu.make_async_copy(
                    source_ref.at[
                        pl.ds(first, height), pl.ds(pl.multiple_of(block * BLOCK, BLOCK), BLOCK)
                    ],
                    target.at[:, pl.ds(i * BLOCK, BLOCK)],
                    sem.at[len(copies)],
                )
            )
    for copy in copies:
        copy.start()
    for copy in copies:
        copy.wait()
    place = index_ref[SLOTS]

    def dot(ahead, piece):
        start = pl.multiple_of(lax.rem(place + ahead, 4) * SHARE, SHARE)
        return lax.dot_general(
            scaled_ref[:, pl.ds(start, SHARE)], piece[...], LAST, preferred_element_type=f32
        )

    far = jnp.concatenate([dot(2, far_a), dot(2, far_b)], axis=1)
    fit = (dot(0, own) + dot(1, right) + far + dot(3, left) - shift_ref[...]).astype(bf16)
    for x in range(4):
        fit_ref[x] = fit


def pick_blocks(index, dosage, scaled, shift):
    tall = jax.ShapeDtypeStruct((ROWS, SHARE), bf16)
    flat = jax.ShapeDtypeStruct((PART, SHARE), bf16)
    return pl.pallas_call(
        pick_kernel,
        in_specs=[
            pl.BlockSpec(memory_space=pltpu.SMEM),
            pl.BlockSpec(memory_space=pl.ANY),
            WHOLE,
            WHOLE,
        ],
        out_specs=[WHOLE] * 6,
        out_shape=[tall, tall, flat, flat, tall, jax.ShapeDtypeStruct((4, FITS, ROWS), bf16)],
        scratch_shapes=[pltpu.SemaphoreType.DMA((5 * EACH,))],
        name="pick_blocks",
    )(index, dosage, scaled, shift)


def send_gradient(residual, center_ref, pieces, extra_ref, out_ref):
    sums = jnp.sum(residual.astype(f32), axis=1, keepdims=True)

    def dot(piece, first, height):
        return jnp.dot(
            residual[:, first : first + height], piece[...], preferred_element_type=f32
        )

    def half(group, first):
        own, right, far_a, far_b, left = group
        far = dot(far_a, first, PART) + dot(far_b, first + PART, PART)
        return [dot(own, first, ROWS), dot(right, first, ROWS), far, dot(left, first, ROWS)]

    both = zip(half(pieces[:5], 0), half(pieces[5:], ROWS))
    for j, (near, other) in enumerate(both):
        lane = pl.ds(j * SHARE, SHARE)
        piece = (near + other - center_ref[:, lane] * sums).astype(bf16)
        for y in range(4):
            out_ref[y, :, lane] = piece
    if extra_ref is not None:
        for y in range(4):
            out_ref[y, :, NS:] = extra_ref[...]


def first_kernel(residual_ref, center_ref, *refs):
    send_gradient(residual_ref[...], center_ref, refs[:10], None, refs[10])


def first_sweep(residual, center, pieces):
    return pl.pallas_call(
        first_kernel,
        in_specs=[WHOLE] * 12,
        out_specs=WHOLE,
        out_shape=jax.ShapeDtypeStruct((4, OWN, NS), bf16),
        name="first_sweep",
    )(residual, center, *pieces)


def middle_kernel(got_ref, out_ref):
    total = got_ref[0, :, :NS].astype(f32)
    for y in range(1, 4):
        total = total + got_ref[y, :, :NS].astype(f32)
    total = total.astype(bf16)
    for z in range(8):
        out_ref[z, :, :NS] = total
        if got_ref.shape[2] > NS:
            for y in range(4):
                out_ref[z, :, NS + y * PEAK : NS + (y + 1) * PEAK] = got_ref[y, :, NS:]


def middle(got):
    width = NS + 4 * (got.shape[2] - NS)
    return pl.pallas_call(
        middle_kernel,
        in_specs=[WHOLE],
        out_specs=WHOLE,
        out_shape=jax.ShapeDtypeStruct((8, OWN, width), bf16),
        name="middle",
    )(got)


def prox(got_ref, point, previous, scale, column_ref, factor):
    total = got_ref[0, :, :NS].astype(f32)
    for z in range(1, 8):
        total = total + got_ref[z, :, :NS].astype(f32)
    step, threshold, counts = (column_ref[:, i : i + 1] for i in range(3))
    moved = point + step * (scale * total / counts)
    current = moved - jnp.clip(moved, -threshold, threshold)
    return current + factor * (current - previous), current


def sweep_kernel(factor, has_extra, *refs):
    got_ref, point_ref, previous_ref, scale_ref, center_ref, column_ref, near_ref = refs[:7]
    pieces = refs[7:17]
    extra_ref = refs[17] if has_extra else None
    out_ref, next_ref, current_ref = refs[-3:]
    scale = scale_ref[...]
    point, current = prox(got_ref, point_ref[...], previous_ref[...], scale, column_ref, factor)
    next_ref[...] = point
    current_ref[...] = current
    weighted = scale * point
    shift = jnp.sum(center_ref[...] * weighted, axis=1, keepdims=True)
    scaled = weighted.astype(bf16)

    def dot(turn, piece):
        return lax.dot_general(
            scaled[:, turn * SHARE : (turn + 1) * SHARE],
            piece[...],
            LAST,
            preferred_element_type=f32,
        )

    def half(group):
        own, right, far_a, far_b, left = group
        far = jnp.concatenate([dot(2, far_a), dot(2, far_b)], axis=1)
        return dot(0, own) + dot(1, right) + far + dot(3, left)

    fitted = jnp.concatenate([half(pieces[:5]), half(pieces[5:])], axis=1) - shift
    residual = (near_ref[1:] * (near_ref[:1] - fitted)).astype(bf16)
    send_gradient(residual, center_ref, pieces, extra_ref, out_ref)


def sweep(factor, extra, *operands):
    width = NS if extra is None else NS + PEAK
    state = jax.ShapeDtypeStruct((OWN, NS), f32)
    more = () if extra is None else (extra,)
    return pl.pallas_call(
        functools.partial(sweep_kernel, factor, extra is not None),
        in_specs=[WHOLE] * (len(operands) + len(more)),
        out_specs=[WHOLE] * 3,
        out_shape=[jax.ShapeDtypeStruct((4, OWN, width), bf16), state, state],
        name="sweep",
    )(*operands, *more)


def last_kernel(got_ref, point_ref, previous_ref, scale_ref, column_ref, out_ref):
    current = prox(got_ref, point_ref[...], previous_ref[...], scale_ref[...], column_ref, 0.0)[1]
    for turn in range(4):
        piece = current[:, turn * SHARE : (turn + 1) * SHARE]
        out_ref[turn] = piece
        out_ref[turn + 4] = piece


def last(got, point, previous, scale, columns):
    return pl.pallas_call(
        last_kernel,
        in_specs=[WHOLE] * 5,
        out_specs=WHOLE,
        out_shape=jax.ShapeDtypeStruct((8, OWN, SHARE), f32),
        name="last",
    )(got, point, previous, scale, columns)


def exchange(value, axis):
    return lax.all_to_all(value, axis, 0, 0, tiled=True)


def swap(value):
    return lax.ppermute(value, "core", [(0, 1), (1, 0)])


def onward(value):
    return lax.ppermute(value, "x", [(i, (i + 1) % 4) for i in range(4)])


def backward(value):
    return lax.ppermute(value, "x", [(i, (i + 3) % 4) for i in range(4)])


def turned(value, count, axis):
    twice = jnp.concatenate([value, value], axis=axis)
    return lax.dynamic_slice_in_dim(twice, count, value.shape[axis], axis)


def lanes(wide):
    return wide.reshape(wide.shape[0], -1, BLOCK).transpose(1, 0, 2)


def shards(
    dosage, centers, scales, phenotype, fold_ids, strong_blocks, warm_start, penalty, step_size
):
    rows, local_width = dosage.shape
    local_blocks = local_width // BLOCK
    core = lax.axis_index("core")
    place = lax.axis_index("x")
    slot = lax.axis_index(PLANE)
    first_fit = core * HALF + place * OWN
    other_fit = (1 - core) * HALF + place * OWN
    ahead = place * EACH

    relative = strong_blocks - place * local_blocks
    owned = (relative >= 0) & (relative < local_blocks)
    center_rows = centers.reshape(-1, BLOCK)
    scale_rows = scales.reshape(-1, BLOCK)
    strong_centers = center_rows[strong_blocks]
    strong_scales = scale_rows[strong_blocks]
    flat_scales = strong_scales.reshape(1, NS)
    coef_mask = jnp.repeat(owned.astype(f32), BLOCK)[None, :]
    warm = warm_start.T
    masked = (flat_scales * warm) * coef_mask
    scaled = masked.astype(bf16)
    shift = jnp.sum(strong_centers.reshape(1, NS) * masked, axis=1, keepdims=True)
    index = jnp.clip(turned(relative, ahead, 0), 0, local_blocks - 1).astype(jnp.int32)
    index = jnp.concatenate([index, place.astype(jnp.int32)[None]])
    own, right, far_a, far_b, left, fit_part = pick_blocks(index, dosage, scaled, shift)

    samples = jnp.stack([phenotype, fold_ids.astype(f32)])
    samples_other = swap(samples)
    fit_part, far_a, far_b = lax.optimization_barrier((fit_part, far_a, far_b))
    via_left = onward(far_a)
    via_right = backward(far_b)
    fitted = exchange(fit_part, "x")
    fitted, via_left, via_right, right, left = lax.optimization_barrier(
        (fitted, via_left, via_right, right, left)
    )
    from_left = onward(right)
    from_right = backward(left)
    far_a = onward(via_left)
    far_b = backward(via_right)

    fit_folds = (jnp.arange(FITS, dtype=jnp.int32) % FOLDS).astype(f32)
    weights = (samples[1:] != fit_folds[:, None]).astype(f32)
    fitted = jnp.sum(fitted.astype(f32), axis=0)
    residual = (weights * (samples[:1] - fitted)).astype(bf16)
    column_sums = jnp.sum(residual.astype(f32), axis=1, keepdims=True)
    residual_own = lax.dynamic_slice_in_dim(residual, first_fit, OWN, 0)
    residual_other = swap(lax.dynamic_slice_in_dim(residual, other_fit, OWN, 0))
    residual_near = jnp.concatenate([residual_own, residual_other], axis=1)

    local_centers = lax.dynamic_slice_in_dim(centers, place * local_width, local_width, 0)
    local_scales = lax.dynamic_slice_in_dim(scale_rows, place * local_blocks, local_blocks, 0)
    cross = jnp.dot(residual, dosage, preferred_element_type=f32) - (
        local_centers[None, :] * column_sums
    )
    keep = lax.dynamic_slice_in_dim(cross, core * HALF, HALF, 0)
    give = lax.dynamic_slice_in_dim(cross, (1 - core) * HALF, HALF, 0)
    summed = (keep + swap(give.astype(bf16)).astype(f32)).astype(bf16)
    padded = jnp.concatenate(
        [lanes(summed), jnp.zeros((PARTS * MBLK - local_blocks, HALF, BLOCK), bf16)], axis=0
    ).reshape(PARTS, MBLK * HALF, BLOCK)
    near = jnp.concatenate([samples, samples_other], axis=1)
    near_weights = (near[1:] != fit_folds[:FOLDS, None]).astype(f32)
    tally_rows = jnp.zeros((8, BLOCK), f32)
    tally_rows = tally_rows.at[0, :FOLDS].set(jnp.sum(near_weights[:, :rows], axis=1))
    tally_rows = tally_rows.at[1, :FOLDS].set(jnp.sum(near_weights[:, rows:], axis=1))
    message = jnp.concatenate(
        [padded, jnp.broadcast_to(tally_rows.astype(bf16)[None], (PARTS, 8, BLOCK))], axis=1
    )
    owner = jnp.repeat(turned(strong_blocks, ahead, 0)[:EACH] // local_blocks, BLOCK)[None, :]
    wide_scale = turned(strong_scales, ahead, 0).reshape(1, NS)
    wide_center = turned(strong_centers, ahead, 0).reshape(1, NS)
    arrived = exchange(message, PLANE)

    share = jnp.where(owner == (place + 3) % 4, from_left, own)
    share = jnp.where(owner == (place + 1) % 4, from_right, share)
    share = jnp.where(
        owner == (place + 2) % 4, jnp.concatenate([far_a, far_b], axis=0), share
    )
    share_left = onward(share)
    share_right = backward(share)
    share_other = swap(share)
    far_a = onward(share_left[:PART])
    far_b = backward(share_right[PART:])
    strong = [share, share_right, far_a, far_b, share_left]
    strong += [share_other] + [swap(piece) for piece in strong[1:]]
    strong = lax.optimization_barrier(tuple(strong))

    first = jnp.sum(arrived.astype(f32), axis=0)
    edge = MBLK * HALF
    counts = (first[edge] + first[edge + 1])[:FOLDS, None]
    fit_penalty = jnp.repeat(penalty, FOLDS)
    half_penalty = lax.dynamic_slice_in_dim(fit_penalty, core * HALF, HALF, 0)[:, None]
    margin_scales = jnp.concatenate(
        [local_scales, jnp.zeros((PARTS * MBLK - local_blocks, BLOCK), f32)], axis=0
    )
    margin_scales = lax.dynamic_slice_in_dim(margin_scales, slot * MBLK, MBLK, 0)
    kkt = margin_scales[:, None, :] * first[:edge].reshape(MBLK, HALF, BLOCK)
    kkt = kkt / jnp.tile(counts, (HALF // FOLDS, 1))[None]
    peak = jnp.max(jnp.abs(kkt) / half_penalty[None], axis=1).reshape(1, PEAK)
    peak_high = peak.astype(bf16)
    peak_low = (peak - peak_high.astype(f32)).astype(bf16)
    extra = jnp.concatenate([peak_high, peak_low, jnp.zeros((2, PEAK), bf16)], axis=0)

    step = lax.dynamic_slice_in_dim(step_size, first_fit, OWN, 0)[:, None]
    threshold = step * lax.dynamic_slice_in_dim(fit_penalty, first_fit, OWN, 0)[:, None]
    columns = jnp.concatenate([step, threshold, counts], axis=1)
    near = jnp.concatenate([near[:1], near_weights], axis=0)
    start = lax.dynamic_slice_in_dim(warm, first_fit, OWN, 0).reshape(OWN, SLOTS, BLOCK)
    point = turned(start, ahead, 1).reshape(OWN, NS)
    previous = point

    sent = first_sweep(residual_near, wide_center, strong)
    got = exchange(middle(exchange(sent, "y")), "z")
    momentum = 1.0
    margin = None
    for round in range(1, ITERS):
        following = (1.0 + math.sqrt(1.0 + 4.0 * momentum * momentum)) / 2.0
        factor = (momentum - 1.0) / following
        sent, point, previous = sweep(
            factor,
            extra if round == 1 else None,
            got,
            point,
            previous,
            wide_scale,
            wide_center,
            columns,
            near,
            *strong,
        )
        got = exchange(middle(exchange(sent, "y")), "z")
        momentum = following
        if round == 1:
            peaks = got[:, :2, NS:].astype(f32)
            peaks = jnp.sum(peaks, axis=1).reshape(PARTS * PEAK)[:local_width]
            margin = jnp.maximum(peaks, swap(peaks))
    leaving = last(got, point, previous, wide_scale, columns)
    leaving = turned(leaving[:4], (4 - place) % 4, 0)
    landed = exchange(jnp.concatenate([leaving, leaving], axis=0), ("core", "x"))
    return (margin, landed.reshape(FITS, SHARE).T)


def solution(mesh):
    cube = Mesh(mesh.devices.reshape(8, 4, 2, 4), ("z", "y", "core", "x"))
    samp = ("z", "y", "core")
    return jax.shard_map(
        shards,
        mesh=cube,
        in_specs=(P(samp, "x"), P(), P(), P(samp), P(samp), P(), P(), P(), P()),
        out_specs=(P("x"), P("x", None)),
        check_vma=False,
    )
```

```python
import functools
import math

import jax
import jax.numpy as jnp
from jax import lax
from jax.experimental import pallas as pl
from jax.experimental.pallas import tpu as pltpu
from jax.sharding import Mesh
from jax.sharding import PartitionSpec as P

BLOCK = 128
SLOTS = 32
NS = SLOTS * BLOCK
LAMBDAS = 8
FOLDS = 4
FITS = LAMBDAS * FOLDS
HALF = FITS // 2
OWN = 4
SHARE = NS // 4
EACH = SHARE // BLOCK
ITERS = 3
PLANE = ("z", "y")
PARTS = 32
MBLK = 3
ROWS = 256
PART = ROWS // 2
PEAK = MBLK * BLOCK

f32 = jnp.float32
bf16 = jnp.bfloat16
LAST = (((1,), (1,)), ((), ()))
WHOLE = pl.BlockSpec(memory_space=pltpu.VMEM)
ROOM = pltpu.CompilerParams(vmem_limit_bytes=12 * 2**20)


def pick_kernel(
    block_ref,
    source_ref,
    centers_ref,
    scales_ref,
    warm_ref,
    own,
    right,
    far_a,
    far_b,
    left,
    fit_ref,
    wide_scale_ref,
    wide_center_ref,
    scale_rows,
    center_rows,
    scaled_ref,
    sem,
):
    place = block_ref[SLOTS]
    local_blocks = source_ref.shape[1] // BLOCK
    slots = [lax.rem(place * EACH + r, SLOTS) for r in range(SLOTS)]
    blocks = [block_ref[slot] for slot in slots]
    for r, block in enumerate(blocks):
        pltpu.make_async_copy(scales_ref.at[block], scale_rows.at[r], sem.at[0]).start()
        pltpu.make_async_copy(centers_ref.at[block], center_rows.at[r], sem.at[1]).start()
    relative = [block - place * local_blocks for block in blocks]
    moves = (
        (own, 0, 0, ROWS),
        (right, 1, 0, ROWS),
        (far_a, 2, 0, PART),
        (far_b, 2, PART, PART),
        (left, 3, 0, ROWS),
    )
    for k, (target, turn, first, height) in enumerate(moves):
        for i in range(EACH):
            local = jnp.clip(relative[turn * EACH + i], 0, local_blocks - 1)
            pltpu.make_async_copy(
                source_ref.at[
                    pl.ds(first, height), pl.ds(pl.multiple_of(local * BLOCK, BLOCK), BLOCK)
                ],
                target.at[:, pl.ds(i * BLOCK, BLOCK)],
                sem.at[2 + k],
            ).start()
    pltpu.make_async_copy(scales_ref.at[pl.ds(0, SLOTS)], scale_rows, sem.at[0]).wait()
    pltpu.make_async_copy(centers_ref.at[pl.ds(0, SLOTS)], center_rows, sem.at[1]).wait()
    moments = jnp.zeros((FITS, BLOCK), f32)
    for r in range(SLOTS):
        lane = pl.ds(r * BLOCK, BLOCK)
        scale = scale_rows[r]
        center = center_rows[r]
        wide_scale_ref[:, lane] = scale
        wide_center_ref[:, lane] = center
        mine = (relative[r] >= 0) & (relative[r] < local_blocks)
        coef = warm_ref[:, pl.ds(pl.multiple_of(slots[r] * BLOCK, BLOCK), BLOCK)]
        coef = scale * coef * jnp.where(mine, 1.0, 0.0)
        moments = moments + center * coef
        scaled_ref[:, lane] = coef.astype(bf16)
    shift = jnp.sum(moments, axis=1, keepdims=True)
    for k, (target, turn, first, height) in enumerate(moves):
        pltpu.make_async_copy(
            source_ref.at[pl.ds(0, height), pl.ds(0, SHARE)], target, sem.at[2 + k]
        ).wait()

    def dot(turn, piece):
        return lax.dot_general(
            scaled_ref[:, turn * SHARE : (turn + 1) * SHARE],
            piece[...],
            LAST,
            preferred_element_type=f32,
        )

    far = jnp.concatenate([dot(2, far_a), dot(2, far_b)], axis=1)
    fit = (dot(0, own) + dot(1, right) + far + dot(3, left) - shift).astype(bf16)
    for x in range(4):
        fit_ref[x] = fit


def pick_blocks(blocks, dosage, centers, scales, warm):
    tall = jax.ShapeDtypeStruct((ROWS, SHARE), bf16)
    flat = jax.ShapeDtypeStruct((PART, SHARE), bf16)
    wide = jax.ShapeDtypeStruct((1, NS), f32)
    anywhere = pl.BlockSpec(memory_space=pl.ANY)
    return pl.pallas_call(
        pick_kernel,
        in_specs=[pl.BlockSpec(memory_space=pltpu.SMEM), anywhere, anywhere, anywhere, WHOLE],
        out_specs=[WHOLE] * 8,
        out_shape=[
            tall,
            tall,
            flat,
            flat,
            tall,
            jax.ShapeDtypeStruct((4, FITS, ROWS), bf16),
            wide,
            wide,
        ],
        scratch_shapes=[
            pltpu.VMEM((SLOTS, 1, BLOCK), f32),
            pltpu.VMEM((SLOTS, 1, BLOCK), f32),
            pltpu.VMEM((FITS, NS), bf16),
            pltpu.SemaphoreType.DMA((7,)),
        ],
        compiler_params=ROOM,
        name="pick_blocks",
    )(blocks, dosage, centers, scales, warm)


def send_gradient(residual, center_ref, pieces, extra_ref, out_ref):
    sums = jnp.sum(residual.astype(f32), axis=1, keepdims=True)

    def dot(piece, first, height):
        return jnp.dot(
            residual[:, first : first + height], piece[...], preferred_element_type=f32
        )

    def half(group, first):
        own, right, far_a, far_b, left = group
        far = dot(far_a, first, PART) + dot(far_b, first + PART, PART)
        return [dot(own, first, ROWS), dot(right, first, ROWS), far, dot(left, first, ROWS)]

    both = zip(half(pieces[:5], 0), half(pieces[5:], ROWS))
    for j, (near, other) in enumerate(both):
        lane = pl.ds(j * SHARE, SHARE)
        piece = (near + other - center_ref[:, lane] * sums).astype(bf16)
        for y in range(4):
            out_ref[y, :, lane] = piece
    if extra_ref is not None:
        for y in range(4):
            out_ref[y, :, NS:] = extra_ref[...]


def first_kernel(residual_ref, center_ref, *refs):
    send_gradient(residual_ref[...], center_ref, refs[:10], None, refs[10])


def first_sweep(residual, center, pieces):
    return pl.pallas_call(
        first_kernel,
        in_specs=[WHOLE] * 12,
        out_specs=WHOLE,
        out_shape=jax.ShapeDtypeStruct((4, OWN, NS), bf16),
        compiler_params=ROOM,
        name="first_sweep",
    )(residual, center, *pieces)


def middle_kernel(got_ref, out_ref):
    total = got_ref[0, :, :NS].astype(f32)
    for y in range(1, 4):
        total = total + got_ref[y, :, :NS].astype(f32)
    total = total.astype(bf16)
    for z in range(8):
        out_ref[z, :, :NS] = total
        if got_ref.shape[2] > NS:
            for y in range(4):
                out_ref[z, :, NS + y * PEAK : NS + (y + 1) * PEAK] = got_ref[y, :, NS:]


def middle(got):
    width = NS + 4 * (got.shape[2] - NS)
    return pl.pallas_call(
        middle_kernel,
        in_specs=[WHOLE],
        out_specs=WHOLE,
        out_shape=jax.ShapeDtypeStruct((8, OWN, width), bf16),
        compiler_params=ROOM,
        name="middle",
    )(got)


def prox(got_ref, point, previous, scale, column_ref, factor):
    total = got_ref[0, :, :NS].astype(f32)
    for z in range(1, 8):
        total = total + got_ref[z, :, :NS].astype(f32)
    step, threshold, counts = (column_ref[:, i : i + 1] for i in range(3))
    moved = point + step * (scale * total / counts)
    current = moved - jnp.clip(moved, -threshold, threshold)
    return current + factor * (current - previous), current


def sweep_kernel(factor, has_extra, *refs):
    got_ref, point_ref, previous_ref, scale_ref, center_ref, column_ref, near_ref = refs[:7]
    pieces = refs[7:17]
    extra_ref = refs[17] if has_extra else None
    out_ref, next_ref, current_ref = refs[-3:]
    scale = scale_ref[...]
    point, current = prox(got_ref, point_ref[...], previous_ref[...], scale, column_ref, factor)
    next_ref[...] = point
    current_ref[...] = current
    weighted = scale * point
    shift = jnp.sum(center_ref[...] * weighted, axis=1, keepdims=True)
    scaled = weighted.astype(bf16)

    def dot(turn, piece):
        return lax.dot_general(
            scaled[:, turn * SHARE : (turn + 1) * SHARE],
            piece[...],
            LAST,
            preferred_element_type=f32,
        )

    def half(group):
        own, right, far_a, far_b, left = group
        far = jnp.concatenate([dot(2, far_a), dot(2, far_b)], axis=1)
        return dot(0, own) + dot(1, right) + far + dot(3, left)

    fitted = jnp.concatenate([half(pieces[:5]), half(pieces[5:])], axis=1) - shift
    residual = (near_ref[1:] * (near_ref[:1] - fitted)).astype(bf16)
    send_gradient(residual, center_ref, pieces, extra_ref, out_ref)


def sweep(factor, extra, *operands):
    width = NS if extra is None else NS + PEAK
    state = jax.ShapeDtypeStruct((OWN, NS), f32)
    more = () if extra is None else (extra,)
    return pl.pallas_call(
        functools.partial(sweep_kernel, factor, extra is not None),
        in_specs=[WHOLE] * (len(operands) + len(more)),
        out_specs=[WHOLE] * 3,
        out_shape=[jax.ShapeDtypeStruct((4, OWN, width), bf16), state, state],
        compiler_params=ROOM,
        name="sweep",
    )(*operands, *more)


def last_kernel(place_ref, got_ref, point_ref, previous_ref, scale_ref, column_ref, out_ref):
    current = prox(got_ref, point_ref[...], previous_ref[...], scale_ref[...], column_ref, 0.0)[1]
    for turn in range(4):
        piece = current[:, turn * SHARE : (turn + 1) * SHARE]
        spot = lax.rem(place_ref[0] + turn, 4)
        out_ref[spot] = piece
        out_ref[spot + 4] = piece


def last(place, got, point, previous, scale, columns):
    return pl.pallas_call(
        last_kernel,
        in_specs=[pl.BlockSpec(memory_space=pltpu.SMEM)] + [WHOLE] * 5,
        out_specs=WHOLE,
        out_shape=jax.ShapeDtypeStruct((8, OWN, SHARE), f32),
        compiler_params=ROOM,
        name="last",
    )(place, got, point, previous, scale, columns)


def exchange(value, axis):
    return lax.all_to_all(value, axis, 0, 0, tiled=True)


def swap(value):
    return lax.ppermute(value, "core", [(0, 1), (1, 0)])


def onward(value):
    return lax.ppermute(value, "x", [(i, (i + 1) % 4) for i in range(4)])


def backward(value):
    return lax.ppermute(value, "x", [(i, (i + 3) % 4) for i in range(4)])


def turned(value, count, axis):
    twice = jnp.concatenate([value, value], axis=axis)
    return lax.dynamic_slice_in_dim(twice, count, value.shape[axis], axis)


def lanes(wide):
    return wide.reshape(wide.shape[0], -1, BLOCK).transpose(1, 0, 2)


def shards(
    dosage, centers, scales, phenotype, fold_ids, strong_blocks, warm_start, penalty, step_size
):
    rows, local_width = dosage.shape
    local_blocks = local_width // BLOCK
    core = lax.axis_index("core")
    place = lax.axis_index("x")
    slot = lax.axis_index(PLANE)
    first_fit = core * HALF + place * OWN
    other_fit = (1 - core) * HALF + place * OWN
    ahead = place * EACH

    scale_rows = scales.reshape(-1, BLOCK)
    warm = warm_start.T
    spot = place.astype(jnp.int32)[None]
    own, right, far_a, far_b, left, fit_part, wide_scale, wide_center = pick_blocks(
        jnp.concatenate([strong_blocks, spot]),
        dosage,
        centers.reshape(-1, 1, BLOCK),
        scales.reshape(-1, 1, BLOCK),
        warm,
    )

    samples = jnp.stack([phenotype, fold_ids.astype(f32)])
    samples_other = swap(samples)
    via_left = onward(far_a)
    via_right = backward(far_b)
    from_left = onward(right)
    from_right = backward(left)
    fitted = exchange(fit_part, "x")
    fitted, via_left, via_right = lax.optimization_barrier((fitted, via_left, via_right))
    far_a = onward(via_left)
    far_b = backward(via_right)

    fit_folds = (jnp.arange(FITS, dtype=jnp.int32) % FOLDS).astype(f32)
    weights = (samples[1:] != fit_folds[:, None]).astype(f32)
    fitted = jnp.sum(fitted.astype(f32), axis=0)
    residual = (weights * (samples[:1] - fitted)).astype(bf16)
    column_sums = jnp.sum(residual.astype(f32), axis=1, keepdims=True)
    residual_own = lax.dynamic_slice_in_dim(residual, first_fit, OWN, 0)
    residual_other = swap(lax.dynamic_slice_in_dim(residual, other_fit, OWN, 0))
    residual_near = jnp.concatenate([residual_own, residual_other], axis=1)

    local_centers = lax.dynamic_slice_in_dim(centers, place * local_width, local_width, 0)
    local_scales = lax.dynamic_slice_in_dim(scale_rows, place * local_blocks, local_blocks, 0)
    cross = jnp.dot(residual, dosage, preferred_element_type=f32) - (
        local_centers[None, :] * column_sums
    )
    keep = lax.dynamic_slice_in_dim(cross, core * HALF, HALF, 0)
    give = lax.dynamic_slice_in_dim(cross, (1 - core) * HALF, HALF, 0)
    summed = (keep + swap(give.astype(bf16)).astype(f32)).astype(bf16)
    padded = jnp.concatenate(
        [lanes(summed), jnp.zeros((PARTS * MBLK - local_blocks, HALF, BLOCK), bf16)], axis=0
    ).reshape(PARTS, MBLK * HALF, BLOCK)
    near = jnp.concatenate([samples, samples_other], axis=1)
    near_weights = (near[1:] != fit_folds[:FOLDS, None]).astype(f32)
    tally_rows = jnp.zeros((8, BLOCK), f32)
    tally_rows = tally_rows.at[0, :FOLDS].set(jnp.sum(near_weights[:, :rows], axis=1))
    tally_rows = tally_rows.at[1, :FOLDS].set(jnp.sum(near_weights[:, rows:], axis=1))
    message = jnp.concatenate(
        [padded, jnp.broadcast_to(tally_rows.astype(bf16)[None], (PARTS, 8, BLOCK))], axis=1
    )
    owner = jnp.repeat(turned(strong_blocks, ahead, 0)[:EACH] // local_blocks, BLOCK)[None, :]
    share = jnp.where(owner == (place + 3) % 4, from_left, own)
    share = jnp.where(owner == (place + 1) % 4, from_right, share)
    share = jnp.where(
        owner == (place + 2) % 4, jnp.concatenate([far_a, far_b], axis=0), share
    )
    message, share = lax.optimization_barrier((message, share))
    arrived = exchange(message, PLANE)
    share_left = onward(share)
    share_right = backward(share)
    share_other = swap(share)
    far_a = onward(share_left[:PART])
    far_b = backward(share_right[PART:])
    strong = [share, share_right, far_a, far_b, share_left]
    strong += [share_other] + [swap(piece) for piece in strong[1:]]
    strong = lax.optimization_barrier(tuple(strong))

    first = jnp.sum(arrived.astype(f32), axis=0)
    edge = MBLK * HALF
    counts = (first[edge] + first[edge + 1])[:FOLDS, None]
    fit_penalty = jnp.repeat(penalty, FOLDS)
    half_penalty = lax.dynamic_slice_in_dim(fit_penalty, core * HALF, HALF, 0)[:, None]
    margin_scales = jnp.concatenate(
        [local_scales, jnp.zeros((PARTS * MBLK - local_blocks, BLOCK), f32)], axis=0
    )
    margin_scales = lax.dynamic_slice_in_dim(margin_scales, slot * MBLK, MBLK, 0)
    kkt = margin_scales[:, None, :] * first[:edge].reshape(MBLK, HALF, BLOCK)
    kkt = kkt / jnp.tile(counts, (HALF // FOLDS, 1))[None]
    peak = jnp.max(jnp.abs(kkt) / half_penalty[None], axis=1).reshape(1, PEAK)
    peak_high = peak.astype(bf16)
    peak_low = (peak - peak_high.astype(f32)).astype(bf16)
    extra = jnp.concatenate([peak_high, peak_low, jnp.zeros((2, PEAK), bf16)], axis=0)

    step = lax.dynamic_slice_in_dim(step_size, first_fit, OWN, 0)[:, None]
    threshold = step * lax.dynamic_slice_in_dim(fit_penalty, first_fit, OWN, 0)[:, None]
    columns = jnp.concatenate([step, threshold, counts], axis=1)
    near = jnp.concatenate([near[:1], near_weights], axis=0)
    start = lax.dynamic_slice_in_dim(warm, first_fit, OWN, 0).reshape(OWN, SLOTS, BLOCK)
    point = turned(start, ahead, 1).reshape(OWN, NS)
    previous = point

    sent = first_sweep(residual_near, wide_center, strong)
    got = exchange(middle(exchange(sent, "y")), "z")
    momentum = 1.0
    margin = None
    for round in range(1, ITERS):
        following = (1.0 + math.sqrt(1.0 + 4.0 * momentum * momentum)) / 2.0
        factor = (momentum - 1.0) / following
        sent, point, previous = sweep(
            factor,
            extra if round == 1 else None,
            got,
            point,
            previous,
            wide_scale,
            wide_center,
            columns,
            near,
            *strong,
        )
        got = exchange(middle(exchange(sent, "y")), "z")
        momentum = following
        if round == 1:
            peaks = got[:, :2, NS:].astype(f32)
            peaks = jnp.sum(peaks, axis=1).reshape(PARTS * PEAK)[:local_width]
            margin = jnp.maximum(peaks, swap(peaks))
    leaving = last(spot, got, point, previous, wide_scale, columns)
    landed = exchange(leaving, ("core", "x"))
    return (margin, landed.reshape(FITS, SHARE).T)


def solution(mesh):
    cube = Mesh(mesh.devices.reshape(8, 4, 2, 4), ("z", "y", "core", "x"))
    samp = ("z", "y", "core")
    return jax.shard_map(
        shards,
        mesh=cube,
        in_specs=(P(samp, "x"), P(), P(), P(samp), P(samp), P(), P(), P(), P()),
        out_specs=(P("x"), P("x", None)),
        check_vma=False,
    )
```

```python
import functools
import math

import jax
import jax.numpy as jnp
from jax import lax
from jax.experimental import pallas as pl
from jax.experimental.pallas import tpu as pltpu
from jax.sharding import Mesh
from jax.sharding import PartitionSpec as P

BLOCK = 128
SLOTS = 32
NS = SLOTS * BLOCK
LAMBDAS = 8
FOLDS = 4
FITS = LAMBDAS * FOLDS
HALF = FITS // 2
OWN = 4
SHARE = NS // 4
EACH = SHARE // BLOCK
ITERS = 3
PLANE = ("z", "y")
PARTS = 32
MBLK = 3
ROWS = 256
PART = ROWS // 2
PEAK = MBLK * BLOCK

f32 = jnp.float32
bf16 = jnp.bfloat16
LAST = (((1,), (1,)), ((), ()))
WHOLE = pl.BlockSpec(memory_space=pltpu.VMEM)
ROOM = pltpu.CompilerParams(vmem_limit_bytes=12 * 2**20)


def pick_kernel(
    block_ref,
    source_ref,
    centers_ref,
    scales_ref,
    warm_ref,
    own,
    right,
    far_a,
    far_b,
    left,
    fit_ref,
    wide_ref,
    local_ref,
    state_ref,
    scale_rows,
    center_rows,
    local_rows,
    scaled_ref,
    sem,
):
    place = lax.axis_index("x")
    local_blocks = source_ref.shape[1] // BLOCK
    slots = [lax.rem(place * EACH + r, SLOTS) for r in range(SLOTS)]
    blocks = [block_ref[slot] for slot in slots]
    for r, block in enumerate(blocks):
        pltpu.make_async_copy(scales_ref.at[block], scale_rows.at[r], sem.at[0]).start()
        pltpu.make_async_copy(centers_ref.at[block], center_rows.at[r], sem.at[1]).start()
    pltpu.make_async_copy(
        centers_ref.at[pl.ds(place * local_blocks, local_blocks)], local_rows, sem.at[7]
    ).start()
    relative = [block - place * local_blocks for block in blocks]
    moves = (
        (own, 0, 0, ROWS),
        (right, 1, 0, ROWS),
        (far_a, 2, 0, PART),
        (far_b, 2, PART, PART),
        (left, 3, 0, ROWS),
    )
    for k, (target, turn, first, height) in enumerate(moves):
        for i in range(EACH):
            local = jnp.clip(relative[turn * EACH + i], 0, local_blocks - 1)
            pltpu.make_async_copy(
                source_ref.at[
                    pl.ds(first, height), pl.ds(pl.multiple_of(local * BLOCK, BLOCK), BLOCK)
                ],
                target.at[:, pl.ds(i * BLOCK, BLOCK)],
                sem.at[2 + k],
            ).start()
    pltpu.make_async_copy(scales_ref.at[pl.ds(0, SLOTS)], scale_rows, sem.at[0]).wait()
    pltpu.make_async_copy(centers_ref.at[pl.ds(0, SLOTS)], center_rows, sem.at[1]).wait()
    moments = jnp.zeros((FITS, BLOCK), f32)
    group = lax.axis_index("core") * (HALF // OWN) + place
    for r in range(SLOTS):
        lane = pl.ds(r * BLOCK, BLOCK)
        scale = scale_rows[r]
        center = center_rows[r]
        wide_ref[0:1, lane] = scale
        wide_ref[1:2, lane] = center
        mine = (relative[r] >= 0) & (relative[r] < local_blocks)
        coef = warm_ref[:, pl.ds(pl.multiple_of(slots[r] * BLOCK, BLOCK), BLOCK)]
        start = jnp.zeros((OWN, BLOCK), f32)
        for q in range(FITS // OWN):
            start = jnp.where(group == q, coef[q * OWN : (q + 1) * OWN], start)
        state_ref[:OWN, lane] = start
        state_ref[OWN:, lane] = start
        coef = scale * coef * jnp.where(mine, 1.0, 0.0)
        moments = moments + center * coef
        scaled_ref[:, lane] = coef.astype(bf16)
    shift = jnp.sum(moments, axis=1, keepdims=True)
    pltpu.make_async_copy(
        centers_ref.at[pl.ds(0, local_blocks)], local_rows, sem.at[7]
    ).wait()
    for r in range(local_blocks):
        local_ref[:, r * BLOCK : (r + 1) * BLOCK] = local_rows[r]
    for k, (target, turn, first, height) in enumerate(moves):
        pltpu.make_async_copy(
            source_ref.at[pl.ds(0, height), pl.ds(0, SHARE)], target, sem.at[2 + k]
        ).wait()

    def dot(turn, piece):
        return lax.dot_general(
            scaled_ref[:, turn * SHARE : (turn + 1) * SHARE],
            piece[...],
            LAST,
            preferred_element_type=f32,
        )

    far = jnp.concatenate([dot(2, far_a), dot(2, far_b)], axis=1)
    fit = (dot(0, own) + dot(1, right) + far + dot(3, left) - shift).astype(bf16)
    for x in range(4):
        fit_ref[x] = fit


def pick_blocks(blocks, dosage, centers, scales, warm):
    tall = jax.ShapeDtypeStruct((ROWS, SHARE), bf16)
    flat = jax.ShapeDtypeStruct((PART, SHARE), bf16)
    far = pl.BlockSpec(memory_space=pltpu.HBM)
    return pl.pallas_call(
        pick_kernel,
        in_specs=[pl.BlockSpec(memory_space=pltpu.SMEM), far, far, far, WHOLE],
        out_specs=[WHOLE] * 9,
        out_shape=[
            tall,
            tall,
            flat,
            flat,
            tall,
            jax.ShapeDtypeStruct((4, FITS, ROWS), bf16),
            jax.ShapeDtypeStruct((2, NS), f32),
            jax.ShapeDtypeStruct((1, dosage.shape[1]), f32),
            jax.ShapeDtypeStruct((2 * OWN, NS), f32),
        ],
        scratch_shapes=[
            pltpu.VMEM((SLOTS, 1, BLOCK), f32),
            pltpu.VMEM((SLOTS, 1, BLOCK), f32),
            pltpu.VMEM((dosage.shape[1] // BLOCK, 1, BLOCK), f32),
            pltpu.VMEM((FITS, NS), bf16),
            pltpu.SemaphoreType.DMA((8,)),
        ],
        compiler_params=ROOM,
        name="pick_blocks",
    )(blocks, dosage, centers, scales, warm)


def send_gradient(residuals, wide_ref, pieces, extra_ref, out_ref):
    sums = sum(jnp.sum(part.astype(f32), axis=1, keepdims=True) for part in residuals)

    def half(residual, group):
        own, right, far_a, far_b, left = (piece[...] for piece in group)

        def dot(part, piece):
            return jnp.dot(part, piece, preferred_element_type=f32)

        far = dot(residual[:, :PART], far_a) + dot(residual[:, PART:], far_b)
        return [dot(residual, own), dot(residual, right), far, dot(residual, left)]

    both = zip(half(residuals[0], pieces[:5]), half(residuals[1], pieces[5:]))
    for j, (near, other) in enumerate(both):
        lane = pl.ds(j * SHARE, SHARE)
        piece = (near + other - wide_ref[1:2, lane] * sums).astype(bf16)
        for y in range(4):
            out_ref[y, :, lane] = piece
    if extra_ref is not None:
        for y in range(4):
            out_ref[y, :, NS:] = extra_ref[...]


def first_kernel(residual_ref, other_ref, wide_ref, *refs):
    send_gradient([residual_ref[...], other_ref[...]], wide_ref, refs[:10], None, refs[10])


def first_sweep(residual, other, wide, pieces):
    return pl.pallas_call(
        first_kernel,
        in_specs=[WHOLE] * 13,
        out_specs=WHOLE,
        out_shape=jax.ShapeDtypeStruct((4, OWN, NS), bf16),
        compiler_params=ROOM,
        name="first_sweep",
    )(residual, other, wide, *pieces)


def settle_kernel(
    local_blocks, penalty_ref, step_ref, arrived_ref, scales_ref, extra_ref, column_ref, rows, sem
):
    core = lax.axis_index("core")
    place = lax.axis_index("x")
    slot = lax.axis_index("z") * 4 + lax.axis_index("y")
    for i in range(MBLK):
        block = jnp.minimum(slot * MBLK + i, local_blocks - 1) + place * local_blocks
        pltpu.make_async_copy(scales_ref.at[block], rows.at[i], sem).start()
    first = arrived_ref[0].astype(f32)
    for source in range(1, PARTS):
        first = first + arrived_ref[source].astype(f32)
    edge = MBLK * HALF
    totals = first[edge : edge + 1] + first[edge + 1 : edge + 2]
    row = lax.broadcasted_iota(jnp.int32, (HALF, BLOCK), 0)
    lane = lax.broadcasted_iota(jnp.int32, (HALF, BLOCK), 1)
    counts = jnp.sum(jnp.where(lane == row % FOLDS, totals, 0.0), axis=1, keepdims=True)
    limit = jnp.zeros((HALF, BLOCK), f32)
    for q in range(HALF // FOLDS):
        limit = jnp.where(row // FOLDS == q, penalty_ref[core * (HALF // FOLDS) + q], limit)
    pltpu.make_async_copy(scales_ref.at[pl.ds(0, MBLK)], rows, sem).wait()
    few = lax.broadcasted_iota(jnp.int32, (OWN, BLOCK), 0)
    for i in range(MBLK):
        kkt = rows[i] * first[i * HALF : (i + 1) * HALF] / counts
        peak = jnp.max(jnp.abs(kkt) / limit, axis=0, keepdims=True)
        high = peak.astype(bf16).astype(f32)
        both = jnp.where(few == 0, high, jnp.where(few == 1, peak - high, 0.0))
        extra_ref[:, i * BLOCK : (i + 1) * BLOCK] = both.astype(bf16)
    step = jnp.zeros((OWN, BLOCK), f32)
    for j in range(OWN):
        step = jnp.where(few == j, step_ref[core * HALF + place * OWN + j], step)
    threshold = step * penalty_ref[core * (HALF // FOLDS) + place]
    few_lane = lane[:OWN]
    column_ref[...] = jnp.where(
        few_lane == 0, step, jnp.where(few_lane == 1, threshold, counts[:OWN])
    )


def settle(local_blocks, penalty, step_size, arrived, scales):
    small = pl.BlockSpec(memory_space=pltpu.SMEM)
    return pl.pallas_call(
        functools.partial(settle_kernel, local_blocks),
        in_specs=[small, small, WHOLE, pl.BlockSpec(memory_space=pltpu.HBM)],
        out_specs=[WHOLE] * 2,
        out_shape=[
            jax.ShapeDtypeStruct((OWN, PEAK), bf16),
            jax.ShapeDtypeStruct((OWN, BLOCK), f32),
        ],
        scratch_shapes=[pltpu.VMEM((MBLK, 1, BLOCK), f32), pltpu.SemaphoreType.DMA],
        compiler_params=ROOM,
        name="settle",
    )(penalty, step_size, arrived, scales)


def middle_kernel(got_ref, out_ref):
    total = got_ref[0, :, :NS].astype(f32)
    for y in range(1, 4):
        total = total + got_ref[y, :, :NS].astype(f32)
    total = total.astype(bf16)
    for z in range(8):
        out_ref[z, :, :NS] = total
        if got_ref.shape[2] > NS:
            for y in range(4):
                out_ref[z, :, NS + y * PEAK : NS + (y + 1) * PEAK] = got_ref[y, :, NS:]


def middle(got):
    width = NS + 4 * (got.shape[2] - NS)
    return pl.pallas_call(
        middle_kernel,
        in_specs=[WHOLE],
        out_specs=WHOLE,
        out_shape=jax.ShapeDtypeStruct((8, OWN, width), bf16),
        compiler_params=ROOM,
        name="middle",
    )(got)


def prox(got_ref, state_ref, wide_ref, column_ref, factor):
    total = got_ref[0, :, :NS].astype(f32)
    for z in range(1, 8):
        total = total + got_ref[z, :, :NS].astype(f32)
    step, threshold, counts = (column_ref[:, i : i + 1] for i in range(3))
    moved = state_ref[:OWN] + step * (wide_ref[0:1] * total / counts)
    current = moved - jnp.clip(moved, -threshold, threshold)
    return current + factor * (current - state_ref[OWN:]), current


def sweep_kernel(factor, has_extra, *refs):
    got_ref, state_ref, wide_ref, column_ref, samples_ref, other_ref = refs[:6]
    pieces = refs[6:16]
    extra_ref = refs[16] if has_extra else None
    out_ref, next_ref = refs[-2:]
    point, current = prox(got_ref, state_ref, wide_ref, column_ref, factor)
    next_ref[:OWN] = point
    next_ref[OWN:] = current
    weighted = wide_ref[0:1] * point
    shift = jnp.sum(wide_ref[1:2] * weighted, axis=1, keepdims=True)
    scaled = weighted.astype(bf16)

    def dot(turn, piece):
        return lax.dot_general(
            scaled[:, turn * SHARE : (turn + 1) * SHARE],
            piece[...],
            LAST,
            preferred_element_type=f32,
        )

    def half(ref, group):
        own, right, far_a, far_b, left = group
        far = jnp.concatenate([dot(2, far_a), dot(2, far_b)], axis=1)
        fitted = dot(0, own) + dot(1, right) + far + dot(3, left) - shift
        fold = lax.broadcasted_iota(jnp.int32, (OWN, ROWS), 0).astype(f32)
        weight = jnp.where(ref[1:2] != fold, 1.0, 0.0)
        return (weight * (ref[0:1] - fitted)).astype(bf16)

    residuals = [half(samples_ref, pieces[:5]), half(other_ref, pieces[5:])]
    send_gradient(residuals, wide_ref, pieces, extra_ref, out_ref)


def sweep(factor, extra, *operands):
    width = NS if extra is None else NS + PEAK
    more = () if extra is None else (extra,)
    return pl.pallas_call(
        functools.partial(sweep_kernel, factor, extra is not None),
        in_specs=[WHOLE] * (len(operands) + len(more)),
        out_specs=[WHOLE] * 2,
        out_shape=[
            jax.ShapeDtypeStruct((4, OWN, width), bf16),
            jax.ShapeDtypeStruct((2 * OWN, NS), f32),
        ],
        compiler_params=ROOM,
        name="sweep",
    )(*operands, *more)


def last_kernel(got_ref, state_ref, wide_ref, column_ref, out_ref):
    current = prox(got_ref, state_ref, wide_ref, column_ref, 0.0)[1]
    for turn in range(4):
        piece = current[:, turn * SHARE : (turn + 1) * SHARE]
        spot = lax.rem(lax.axis_index("x") + turn, 4)
        out_ref[spot] = piece
        out_ref[spot + 4] = piece


def last(got, state, wide, columns):
    return pl.pallas_call(
        last_kernel,
        in_specs=[WHOLE] * 4,
        out_specs=WHOLE,
        out_shape=jax.ShapeDtypeStruct((8, OWN, SHARE), f32),
        compiler_params=ROOM,
        name="last",
    )(got, state, wide, columns)


def exchange(value, axis):
    return lax.all_to_all(value, axis, 0, 0, tiled=True)


def swap(value):
    return lax.ppermute(value, "core", [(0, 1), (1, 0)])


def onward(value):
    return lax.ppermute(value, "x", [(i, (i + 1) % 4) for i in range(4)])


def backward(value):
    return lax.ppermute(value, "x", [(i, (i + 3) % 4) for i in range(4)])


def turned(value, count, axis):
    twice = jnp.concatenate([value, value], axis=axis)
    return lax.dynamic_slice_in_dim(twice, count, value.shape[axis], axis)


def lanes(wide):
    return wide.reshape(wide.shape[0], -1, BLOCK).transpose(1, 0, 2)


def shards(
    dosage, centers, scales, phenotype, fold_ids, strong_blocks, warm_start, penalty, step_size
):
    rows, local_width = dosage.shape
    local_blocks = local_width // BLOCK
    core = lax.axis_index("core")
    place = lax.axis_index("x")
    first_fit = core * HALF + place * OWN
    other_fit = (1 - core) * HALF + place * OWN
    ahead = place * EACH

    warm = warm_start.T
    scale_rows = scales.reshape(-1, 1, BLOCK)
    own, right, far_a, far_b, left, fit_part, wide, local_centers, state = pick_blocks(
        strong_blocks, dosage, centers.reshape(-1, 1, BLOCK), scale_rows, warm
    )

    fit_part, phenotype, fold_ids = lax.optimization_barrier((fit_part, phenotype, fold_ids))
    samples = jnp.stack([phenotype, fold_ids.astype(f32)])
    samples_other = swap(samples)
    via_left = onward(far_a)
    via_right = backward(far_b)
    from_left = onward(right)
    from_right = backward(left)
    fitted = exchange(fit_part, "x")
    fitted, via_left, via_right = lax.optimization_barrier((fitted, via_left, via_right))
    far_a = onward(via_left)
    far_b = backward(via_right)

    fit_folds = (jnp.arange(FITS, dtype=jnp.int32) % FOLDS).astype(f32)
    weights = (samples[1:] != fit_folds[:, None]).astype(f32)
    fitted = jnp.sum(fitted.astype(f32), axis=0)
    residual = (weights * (samples[:1] - fitted)).astype(bf16)
    column_sums = jnp.sum(residual.astype(f32), axis=1, keepdims=True)
    residual_own = lax.dynamic_slice_in_dim(residual, first_fit, OWN, 0)
    residual_other = swap(lax.dynamic_slice_in_dim(residual, other_fit, OWN, 0))

    cross = jnp.dot(residual, dosage, preferred_element_type=f32) - (
        local_centers * column_sums
    )
    keep = lax.dynamic_slice_in_dim(cross, core * HALF, HALF, 0)
    give = lax.dynamic_slice_in_dim(cross, (1 - core) * HALF, HALF, 0)
    summed = (keep + swap(give.astype(bf16)).astype(f32)).astype(bf16)
    padded = jnp.concatenate(
        [lanes(summed), jnp.zeros((PARTS * MBLK - local_blocks, HALF, BLOCK), bf16)], axis=0
    ).reshape(PARTS, MBLK * HALF, BLOCK)
    near = jnp.concatenate([samples, samples_other], axis=1)
    near_weights = (near[1:] != fit_folds[:FOLDS, None]).astype(f32)
    tally_rows = jnp.zeros((8, BLOCK), f32)
    tally_rows = tally_rows.at[0, :FOLDS].set(jnp.sum(near_weights[:, :rows], axis=1))
    tally_rows = tally_rows.at[1, :FOLDS].set(jnp.sum(near_weights[:, rows:], axis=1))
    message = jnp.concatenate(
        [padded, jnp.broadcast_to(tally_rows.astype(bf16)[None], (PARTS, 8, BLOCK))], axis=1
    )
    owner = jnp.repeat(turned(strong_blocks, ahead, 0)[:EACH] // local_blocks, BLOCK)[None, :]
    share = jnp.where(owner == (place + 3) % 4, from_left, own)
    share = jnp.where(owner == (place + 1) % 4, from_right, share)
    share = jnp.where(
        owner == (place + 2) % 4, jnp.concatenate([far_a, far_b], axis=0), share
    )
    arrived = exchange(message, PLANE)
    share_left = onward(share)
    share_right = backward(share)
    share_other = swap(share)
    far_a = onward(share_left[:PART])
    far_b = backward(share_right[PART:])
    strong = [share, share_right, far_a, far_b, share_left]
    strong += [share_other] + [swap(piece) for piece in strong[1:]]
    strong = lax.optimization_barrier(tuple(strong))

    sent = first_sweep(residual_own, residual_other, wide, strong)
    sent, arrived = lax.optimization_barrier((sent, arrived))
    extra, columns = settle(local_blocks, penalty, step_size, arrived, scale_rows)

    got = exchange(middle(exchange(sent, "y")), "z")
    momentum = 1.0
    margin = None
    for round in range(1, ITERS):
        following = (1.0 + math.sqrt(1.0 + 4.0 * momentum * momentum)) / 2.0
        factor = (momentum - 1.0) / following
        sent, state = sweep(
            factor,
            extra if round == 1 else None,
            got,
            state,
            wide,
            columns,
            samples,
            samples_other,
            *strong,
        )
        got = exchange(middle(exchange(sent, "y")), "z")
        momentum = following
        if round == 1:
            peaks = got[:, :2, NS:].astype(f32)
            peaks = jnp.sum(peaks, axis=1).reshape(PARTS * PEAK)[:local_width]
            margin = jnp.maximum(peaks, swap(peaks))
    leaving = last(got, state, wide, columns)
    landed = exchange(leaving, ("core", "x"))
    return (margin, landed.reshape(FITS, SHARE).T)


def solution(mesh):
    cube = Mesh(mesh.devices.reshape(8, 4, 2, 4), ("z", "y", "core", "x"))
    samp = ("z", "y", "core")
    return jax.shard_map(
        shards,
        mesh=cube,
        in_specs=(P(samp, "x"), P(), P(), P(samp), P(samp), P(), P(), P(), P()),
        out_specs=(P("x"), P("x", None)),
        check_vma=False,
    )
```

```python
import functools
import math

import jax
import jax.numpy as jnp
from jax import lax
from jax.experimental import pallas as pl
from jax.experimental.pallas import tpu as pltpu
from jax.sharding import Mesh
from jax.sharding import PartitionSpec as P


BLOCK = 128
SLOTS = 32
NS = SLOTS * BLOCK
LAMBDAS = 8
FOLDS = 4
FITS = LAMBDAS * FOLDS
HALF = FITS // 2
OWN = 4
SHARE = NS // 4
EACH = SHARE // BLOCK
ITERS = 3
PLANE = ("z", "y")
PARTS = 32
MBLK = 3
ROWS = 256
PART = ROWS // 2
PEAK = MBLK * BLOCK

f32 = jnp.float32
bf16 = jnp.bfloat16
LAST = (((1,), (1,)), ((), ()))
WHOLE = pl.BlockSpec(memory_space=pltpu.VMEM)
ROOM = pltpu.CompilerParams(vmem_limit_bytes=12 * 2**20)


def pick_kernel(
    block_ref,
    source_ref,
    centers_ref,
    scales_ref,
    source_warm_ref,
    own,
    right,
    far_a,
    far_b,
    left,
    fit_ref,
    wide_ref,
    local_ref,
    state_ref,
    scale_rows,
    center_rows,
    local_rows,
    scaled_ref,
    warm_ref,
    sem,
):
    place = lax.axis_index("x")
    local_blocks = source_ref.shape[1] // BLOCK
    slots = [lax.rem(place * EACH + r, SLOTS) for r in range(SLOTS)]
    blocks = [block_ref[slot] for slot in slots]
    warm_copy = pltpu.make_async_copy(source_warm_ref, warm_ref, sem.at[8])
    warm_copy.start()
    for r, block in enumerate(blocks):
        pltpu.make_async_copy(scales_ref.at[block], scale_rows.at[r], sem.at[0]).start()
        pltpu.make_async_copy(centers_ref.at[block], center_rows.at[r], sem.at[1]).start()
    pltpu.make_async_copy(
        centers_ref.at[pl.ds(place * local_blocks, local_blocks)], local_rows, sem.at[7]
    ).start()
    relative = [block - place * local_blocks for block in blocks]
    moves = (
        (own, 0, 0, ROWS),
        (right, 1, 0, ROWS),
        (far_a, 2, 0, PART),
        (far_b, 2, PART, PART),
        (left, 3, 0, ROWS),
    )
    for k, (target, turn, first, height) in enumerate(moves):
        for i in range(EACH):
            local = jnp.clip(relative[turn * EACH + i], 0, local_blocks - 1)
            pltpu.make_async_copy(
                source_ref.at[
                    pl.ds(first, height), pl.ds(pl.multiple_of(local * BLOCK, BLOCK), BLOCK)
                ],
                target.at[:, pl.ds(i * BLOCK, BLOCK)],
                sem.at[2 + k],
            ).start()
    pltpu.make_async_copy(scales_ref.at[pl.ds(0, SLOTS)], scale_rows, sem.at[0]).wait()
    pltpu.make_async_copy(centers_ref.at[pl.ds(0, SLOTS)], center_rows, sem.at[1]).wait()
    warm_copy.wait()
    moments = jnp.zeros((FITS, BLOCK), f32)
    group = lax.axis_index("core") * (HALF // OWN) + place
    for r in range(SLOTS):
        lane = pl.ds(r * BLOCK, BLOCK)
        scale = scale_rows[r]
        center = center_rows[r]
        wide_ref[0:1, lane] = scale
        wide_ref[1:2, lane] = center
        mine = (relative[r] >= 0) & (relative[r] < local_blocks)
        coef = warm_ref[:, pl.ds(pl.multiple_of(slots[r] * BLOCK, BLOCK), BLOCK)]
        start = jnp.zeros((OWN, BLOCK), f32)
        for q in range(FITS // OWN):
            start = jnp.where(group == q, coef[q * OWN : (q + 1) * OWN], start)
        state_ref[:OWN, lane] = start
        state_ref[OWN:, lane] = start
        coef = scale * coef * jnp.where(mine, 1.0, 0.0)
        moments = moments + center * coef
        scaled_ref[:, lane] = coef.astype(bf16)
    shift = jnp.sum(moments, axis=1, keepdims=True)
    pltpu.make_async_copy(
        centers_ref.at[pl.ds(0, local_blocks)], local_rows, sem.at[7]
    ).wait()
    for r in range(local_blocks):
        local_ref[:, r * BLOCK : (r + 1) * BLOCK] = local_rows[r]
    for k, (target, turn, first, height) in enumerate(moves):
        pltpu.make_async_copy(
            source_ref.at[pl.ds(0, height), pl.ds(0, SHARE)], target, sem.at[2 + k]
        ).wait()

    def dot(turn, piece):
        return lax.dot_general(
            scaled_ref[:, turn * SHARE : (turn + 1) * SHARE],
            piece[...],
            LAST,
            preferred_element_type=f32,
        )

    far = jnp.concatenate([dot(2, far_a), dot(2, far_b)], axis=1)
    fit = (dot(0, own) + dot(1, right) + far + dot(3, left) - shift).astype(bf16)
    for x in range(4):
        fit_ref[x] = fit


def pick_blocks(blocks, dosage, centers, scales, warm):
    tall = jax.ShapeDtypeStruct((ROWS, SHARE), bf16)
    flat = jax.ShapeDtypeStruct((PART, SHARE), bf16)
    far = pl.BlockSpec(memory_space=pltpu.HBM)
    return pl.pallas_call(
        pick_kernel,
        in_specs=[pl.BlockSpec(memory_space=pltpu.SMEM), far, far, far, far],
        out_specs=[WHOLE] * 9,
        out_shape=[
            tall,
            tall,
            flat,
            flat,
            tall,
            jax.ShapeDtypeStruct((4, FITS, ROWS), bf16),
            jax.ShapeDtypeStruct((2, NS), f32),
            jax.ShapeDtypeStruct((1, dosage.shape[1]), f32),
            jax.ShapeDtypeStruct((2 * OWN, NS), f32),
        ],
        scratch_shapes=[
            pltpu.VMEM((SLOTS, 1, BLOCK), f32),
            pltpu.VMEM((SLOTS, 1, BLOCK), f32),
            pltpu.VMEM((dosage.shape[1] // BLOCK, 1, BLOCK), f32),
            pltpu.VMEM((FITS, NS), bf16),
            pltpu.VMEM((FITS, NS), f32),
            pltpu.SemaphoreType.DMA((9,)),
        ],
        name="pick_blocks",
    )(blocks, dosage, centers, scales, warm)


def send_gradient(residuals, wide_ref, pieces, extra_ref, out_ref):
    sums = sum(jnp.sum(part.astype(f32), axis=1, keepdims=True) for part in residuals)

    def half(residual, group):
        own, right, far_a, far_b, left = (piece[...] for piece in group)

        def dot(part, piece):
            return jnp.dot(part, piece, preferred_element_type=f32)

        far = dot(residual[:, :PART], far_a) + dot(residual[:, PART:], far_b)
        return [dot(residual, own), dot(residual, right), far, dot(residual, left)]

    both = zip(half(residuals[0], pieces[:5]), half(residuals[1], pieces[5:]))
    for j, (near, other) in enumerate(both):
        lane = pl.ds(j * SHARE, SHARE)
        piece = (near + other - wide_ref[1:2, lane] * sums).astype(bf16)
        for y in range(4):
            out_ref[y, :, lane] = piece
    if extra_ref is not None:
        for y in range(4):
            out_ref[y, :, NS:] = extra_ref[...]


def first_kernel(residual_ref, other_ref, wide_ref, *refs):
    send_gradient([residual_ref[...], other_ref[...]], wide_ref, refs[:10], None, refs[10])


def first_sweep(residual, other, wide, pieces):
    return pl.pallas_call(
        first_kernel,
        in_specs=[WHOLE] * 13,
        out_specs=WHOLE,
        out_shape=jax.ShapeDtypeStruct((4, OWN, NS), bf16),
        compiler_params=ROOM,
        name="first_sweep",
    )(residual, other, wide, *pieces)


def settle_kernel(
    local_blocks, penalty_ref, step_ref, arrived_ref, scales_ref, extra_ref, column_ref, rows, sem
):
    core = lax.axis_index("core")
    place = lax.axis_index("x")
    slot = lax.axis_index("z") * 4 + lax.axis_index("y")
    for i in range(MBLK):
        block = jnp.minimum(slot * MBLK + i, local_blocks - 1) + place * local_blocks
        pltpu.make_async_copy(scales_ref.at[block], rows.at[i], sem).start()
    first = arrived_ref[0].astype(f32)
    for source in range(1, PARTS):
        first = first + arrived_ref[source].astype(f32)
    edge = MBLK * HALF
    totals = first[edge : edge + 1] + first[edge + 1 : edge + 2]
    row = lax.broadcasted_iota(jnp.int32, (HALF, BLOCK), 0)
    lane = lax.broadcasted_iota(jnp.int32, (HALF, BLOCK), 1)
    counts = jnp.sum(jnp.where(lane == row % FOLDS, totals, 0.0), axis=1, keepdims=True)
    limit = jnp.zeros((HALF, BLOCK), f32)
    for q in range(HALF // FOLDS):
        limit = jnp.where(row // FOLDS == q, penalty_ref[core * (HALF // FOLDS) + q], limit)
    pltpu.make_async_copy(scales_ref.at[pl.ds(0, MBLK)], rows, sem).wait()
    few = lax.broadcasted_iota(jnp.int32, (OWN, BLOCK), 0)
    for i in range(MBLK):
        kkt = rows[i] * first[i * HALF : (i + 1) * HALF] / counts
        peak = jnp.max(jnp.abs(kkt) / limit, axis=0, keepdims=True)
        high = peak.astype(bf16).astype(f32)
        both = jnp.where(few == 0, high, jnp.where(few == 1, peak - high, 0.0))
        extra_ref[:, i * BLOCK : (i + 1) * BLOCK] = both.astype(bf16)
    step = jnp.zeros((OWN, BLOCK), f32)
    for j in range(OWN):
        step = jnp.where(few == j, step_ref[core * HALF + place * OWN + j], step)
    threshold = step * penalty_ref[core * (HALF // FOLDS) + place]
    few_lane = lane[:OWN]
    column_ref[...] = jnp.where(
        few_lane == 0, step, jnp.where(few_lane == 1, threshold, counts[:OWN])
    )


def settle(local_blocks, penalty, step_size, arrived, scales):
    small = pl.BlockSpec(memory_space=pltpu.SMEM)
    return pl.pallas_call(
        functools.partial(settle_kernel, local_blocks),
        in_specs=[small, small, WHOLE, pl.BlockSpec(memory_space=pltpu.HBM)],
        out_specs=[WHOLE] * 2,
        out_shape=[
            jax.ShapeDtypeStruct((OWN, PEAK), bf16),
            jax.ShapeDtypeStruct((OWN, BLOCK), f32),
        ],
        scratch_shapes=[pltpu.VMEM((MBLK, 1, BLOCK), f32), pltpu.SemaphoreType.DMA],
        compiler_params=ROOM,
        name="settle",
    )(penalty, step_size, arrived, scales)


def middle_kernel(got_ref, out_ref):
    total = got_ref[0, :, :NS].astype(f32)
    for y in range(1, 4):
        total = total + got_ref[y, :, :NS].astype(f32)
    total = total.astype(bf16)
    for z in range(8):
        out_ref[z, :, :NS] = total
        if got_ref.shape[2] > NS:
            for y in range(4):
                out_ref[z, :, NS + y * PEAK : NS + (y + 1) * PEAK] = got_ref[y, :, NS:]


def middle(got):
    width = NS + 4 * (got.shape[2] - NS)
    return pl.pallas_call(
        middle_kernel,
        in_specs=[WHOLE],
        out_specs=WHOLE,
        out_shape=jax.ShapeDtypeStruct((8, OWN, width), bf16),
        compiler_params=ROOM,
        name="middle",
    )(got)


def prox(got_ref, state_ref, wide_ref, column_ref, factor):
    total = got_ref[0, :, :NS].astype(f32)
    for z in range(1, 8):
        total = total + got_ref[z, :, :NS].astype(f32)
    step, threshold, counts = (column_ref[:, i : i + 1] for i in range(3))
    moved = state_ref[:OWN] + step * (wide_ref[0:1] * total / counts)
    current = moved - jnp.clip(moved, -threshold, threshold)
    return current + factor * (current - state_ref[OWN:]), current


def sweep_kernel(factor, has_extra, *refs):
    got_ref, state_ref, wide_ref, column_ref, samples_ref, other_ref = refs[:6]
    pieces = refs[6:16]
    extra_ref = refs[16] if has_extra else None
    out_ref, next_ref = refs[-2:]
    point, current = prox(got_ref, state_ref, wide_ref, column_ref, factor)
    next_ref[:OWN] = point
    next_ref[OWN:] = current
    weighted = wide_ref[0:1] * point
    shift = jnp.sum(wide_ref[1:2] * weighted, axis=1, keepdims=True)
    scaled = weighted.astype(bf16)

    def dot(turn, piece):
        return lax.dot_general(
            scaled[:, turn * SHARE : (turn + 1) * SHARE],
            piece[...],
            LAST,
            preferred_element_type=f32,
        )

    def half(ref, group):
        own, right, far_a, far_b, left = group
        far = jnp.concatenate([dot(2, far_a), dot(2, far_b)], axis=1)
        fitted = dot(0, own) + dot(1, right) + far + dot(3, left) - shift
        fold = lax.broadcasted_iota(jnp.int32, (OWN, ROWS), 0).astype(f32)
        weight = jnp.where(ref[1:2] != fold, 1.0, 0.0)
        return (weight * (ref[0:1] - fitted)).astype(bf16)

    residuals = [half(samples_ref, pieces[:5]), half(other_ref, pieces[5:])]
    send_gradient(residuals, wide_ref, pieces, extra_ref, out_ref)


def sweep(factor, extra, *operands):
    width = NS if extra is None else NS + PEAK
    more = () if extra is None else (extra,)
    return pl.pallas_call(
        functools.partial(sweep_kernel, factor, extra is not None),
        in_specs=[WHOLE] * (len(operands) + len(more)),
        out_specs=[WHOLE] * 2,
        out_shape=[
            jax.ShapeDtypeStruct((4, OWN, width), bf16),
            jax.ShapeDtypeStruct((2 * OWN, NS), f32),
        ],
        compiler_params=ROOM,
        name="sweep",
    )(*operands, *more)


def last_kernel(got_ref, state_ref, wide_ref, column_ref, out_ref):
    current = prox(got_ref, state_ref, wide_ref, column_ref, 0.0)[1]
    for turn in range(4):
        piece = current[:, turn * SHARE : (turn + 1) * SHARE]
        spot = lax.rem(lax.axis_index("x") + turn, 4)
        out_ref[spot] = piece
        out_ref[spot + 4] = piece


def last(got, state, wide, columns):
    return pl.pallas_call(
        last_kernel,
        in_specs=[WHOLE] * 4,
        out_specs=WHOLE,
        out_shape=jax.ShapeDtypeStruct((8, OWN, SHARE), f32),
        compiler_params=ROOM,
        name="last",
    )(got, state, wide, columns)


def exchange(value, axis):
    return lax.all_to_all(value, axis, 0, 0, tiled=True)


def swap(value):
    return lax.ppermute(value, "core", [(0, 1), (1, 0)])


def onward(value):
    return lax.ppermute(value, "x", [(i, (i + 1) % 4) for i in range(4)])


def backward(value):
    return lax.ppermute(value, "x", [(i, (i + 3) % 4) for i in range(4)])


def turned(value, count, axis):
    twice = jnp.concatenate([value, value], axis=axis)
    return lax.dynamic_slice_in_dim(twice, count, value.shape[axis], axis)


def lanes(wide):
    return wide.reshape(wide.shape[0], -1, BLOCK).transpose(1, 0, 2)


def shards(
    dosage, centers, scales, phenotype, fold_ids, strong_blocks, warm_start, penalty, step_size
):
    rows, local_width = dosage.shape
    local_blocks = local_width // BLOCK
    core = lax.axis_index("core")
    place = lax.axis_index("x")
    first_fit = core * HALF + place * OWN
    other_fit = (1 - core) * HALF + place * OWN
    ahead = place * EACH

    warm = warm_start.T
    scale_rows = scales.reshape(-1, 1, BLOCK)
    own, right, far_a, far_b, left, fit_part, wide, local_centers, state = pick_blocks(
        strong_blocks, dosage, centers.reshape(-1, 1, BLOCK), scale_rows, warm
    )

    fit_part, phenotype, fold_ids = lax.optimization_barrier((fit_part, phenotype, fold_ids))
    samples = jnp.stack([phenotype, fold_ids.astype(f32)])
    samples_other = swap(samples)
    via_left = onward(far_a)
    via_right = backward(far_b)
    from_left = onward(right)
    from_right = backward(left)
    fitted = exchange(fit_part, "x")
    far_a = onward(via_left)
    far_b = backward(via_right)

    fit_folds = (jnp.arange(FITS, dtype=jnp.int32) % FOLDS).astype(f32)
    weights = (samples[1:] != fit_folds[:, None]).astype(f32)
    fitted = jnp.sum(fitted.astype(f32), axis=0)
    residual = (weights * (samples[:1] - fitted)).astype(bf16)
    column_sums = jnp.sum(residual.astype(f32), axis=1, keepdims=True)
    residual_own = lax.dynamic_slice_in_dim(residual, first_fit, OWN, 0)
    residual_other = swap(lax.dynamic_slice_in_dim(residual, other_fit, OWN, 0))

    cross = jnp.dot(residual, dosage, preferred_element_type=f32) - (
        local_centers * column_sums
    )
    keep = lax.dynamic_slice_in_dim(cross, core * HALF, HALF, 0)
    give = lax.dynamic_slice_in_dim(cross, (1 - core) * HALF, HALF, 0)
    summed = (keep + swap(give.astype(bf16)).astype(f32)).astype(bf16)
    padded = jnp.concatenate(
        [lanes(summed), jnp.zeros((PARTS * MBLK - local_blocks, HALF, BLOCK), bf16)], axis=0
    ).reshape(PARTS, MBLK * HALF, BLOCK)
    near = jnp.concatenate([samples, samples_other], axis=1)
    near_weights = (near[1:] != fit_folds[:FOLDS, None]).astype(f32)
    tally_rows = jnp.zeros((8, BLOCK), f32)
    tally_rows = tally_rows.at[0, :FOLDS].set(jnp.sum(near_weights[:, :rows], axis=1))
    tally_rows = tally_rows.at[1, :FOLDS].set(jnp.sum(near_weights[:, rows:], axis=1))
    message = jnp.concatenate(
        [padded, jnp.broadcast_to(tally_rows.astype(bf16)[None], (PARTS, 8, BLOCK))], axis=1
    )
    owner = jnp.repeat(turned(strong_blocks, ahead, 0)[:EACH] // local_blocks, BLOCK)[None, :]
    share = jnp.where(owner == (place + 3) % 4, from_left, own)
    share = jnp.where(owner == (place + 1) % 4, from_right, share)
    share = jnp.where(owner == (place + 2) % 4, jnp.concatenate([far_a, far_b], axis=0), share)
    arrived = exchange(message, PLANE)
    share_left = onward(share)
    share_right = backward(share)
    share_other = swap(share)
    far_a = onward(share_left[:PART])
    far_b = backward(share_right[PART:])
    strong = [share, share_right, far_a, far_b, share_left]
    strong += [share_other] + [swap(piece) for piece in strong[1:]]
    strong = lax.optimization_barrier(tuple(strong))

    sent = first_sweep(residual_own, residual_other, wide, strong)
    sent, arrived = lax.optimization_barrier((sent, arrived))
    extra, columns = settle(local_blocks, penalty, step_size, arrived, scale_rows)

    got = exchange(middle(exchange(sent, "y")), "z")
    momentum = 1.0
    margin = None
    for round in range(1, ITERS):
        following = (1.0 + math.sqrt(1.0 + 4.0 * momentum * momentum)) / 2.0
        factor = (momentum - 1.0) / following
        sent, state = sweep(
            factor,
            extra if round == 1 else None,
            got,
            state,
            wide,
            columns,
            samples,
            samples_other,
            *strong,
        )
        got = exchange(middle(exchange(sent, "y")), "z")
        momentum = following
        if round == 1:
            peaks = got[:, :2, NS:].astype(f32)
            peaks = jnp.sum(peaks, axis=1).reshape(PARTS * PEAK)[:local_width]
            margin = jnp.maximum(peaks, swap(peaks))
    leaving = last(got, state, wide, columns)
    landed = exchange(leaving, ("core", "x"))
    return (margin, landed.reshape(FITS, SHARE).T)


def solution(mesh):
    cube = Mesh(mesh.devices.reshape(8, 4, 2, 4), ("z", "y", "core", "x"))
    samp = ("z", "y", "core")
    return jax.shard_map(
        shards,
        mesh=cube,
        in_specs=(P(samp, "x"), P(), P(), P(samp), P(samp), P(), P(), P(), P()),
        out_specs=(P("x"), P("x", None)),
        check_vma=False,
    )
```

```python
import functools
import math

import jax
import jax.numpy as jnp
from jax import lax
from jax.experimental import pallas as pl
from jax.experimental.pallas import tpu as pltpu
from jax.sharding import Mesh
from jax.sharding import PartitionSpec as P


BLOCK = 128
SLOTS = 32
NS = SLOTS * BLOCK
LAMBDAS = 8
FOLDS = 4
FITS = LAMBDAS * FOLDS
HALF = FITS // 2
OWN = 4
SHARE = NS // 4
EACH = SHARE // BLOCK
ITERS = 3
PLANE = ("z", "y")
PARTS = 32
MBLK = 3
ROWS = 256
PART = ROWS // 2
PEAK = MBLK * BLOCK

f32 = jnp.float32
bf16 = jnp.bfloat16
LAST = (((1,), (1,)), ((), ()))
WHOLE = pl.BlockSpec(memory_space=pltpu.VMEM)
ROOM = pltpu.CompilerParams(vmem_limit_bytes=12 * 2**20)


def pick_kernel(
    block_ref,
    source_ref,
    centers_ref,
    scales_ref,
    source_warm_ref,
    own,
    right,
    far_a,
    far_b,
    left,
    fit_ref,
    wide_ref,
    local_ref,
    state_ref,
    scale_rows,
    center_rows,
    local_rows,
    scaled_ref,
    warm_ref,
    sem,
):
    place = lax.axis_index("x")
    local_blocks = source_ref.shape[1] // BLOCK
    slots = [lax.rem(place * EACH + r, SLOTS) for r in range(SLOTS)]
    blocks = [block_ref[slot] for slot in slots]
    warm_copy = pltpu.make_async_copy(source_warm_ref, warm_ref, sem.at[8])
    warm_copy.start()
    for r, block in enumerate(blocks):
        pltpu.make_async_copy(scales_ref.at[block], scale_rows.at[r], sem.at[0]).start()
        pltpu.make_async_copy(centers_ref.at[block], center_rows.at[r], sem.at[1]).start()
    pltpu.make_async_copy(
        centers_ref.at[pl.ds(place * local_blocks, local_blocks)], local_rows, sem.at[7]
    ).start()
    relative = [block - place * local_blocks for block in blocks]
    moves = (
        (own, 0, 0, ROWS),
        (right, 1, 0, ROWS),
        (far_a, 2, 0, PART),
        (far_b, 2, PART, PART),
        (left, 3, 0, ROWS),
    )
    for k, (target, turn, first, height) in enumerate(moves):
        for i in range(EACH):
            local = jnp.clip(relative[turn * EACH + i], 0, local_blocks - 1)
            pltpu.make_async_copy(
                source_ref.at[
                    pl.ds(first, height), pl.ds(pl.multiple_of(local * BLOCK, BLOCK), BLOCK)
                ],
                target.at[:, pl.ds(i * BLOCK, BLOCK)],
                sem.at[2 + k],
            ).start()
    pltpu.make_async_copy(scales_ref.at[pl.ds(0, SLOTS)], scale_rows, sem.at[0]).wait()
    pltpu.make_async_copy(centers_ref.at[pl.ds(0, SLOTS)], center_rows, sem.at[1]).wait()
    warm_copy.wait()
    moments = jnp.zeros((FITS, BLOCK), f32)
    group = lax.axis_index("core") * (HALF // OWN) + place
    for r in range(SLOTS):
        lane = pl.ds(r * BLOCK, BLOCK)
        scale = scale_rows[r]
        center = center_rows[r]
        wide_ref[0:1, lane] = scale
        wide_ref[1:2, lane] = center
        mine = (relative[r] >= 0) & (relative[r] < local_blocks)
        coef = warm_ref[:, pl.ds(pl.multiple_of(slots[r] * BLOCK, BLOCK), BLOCK)]
        start = jnp.zeros((OWN, BLOCK), f32)
        for q in range(FITS // OWN):
            start = jnp.where(group == q, coef[q * OWN : (q + 1) * OWN], start)
        state_ref[:OWN, lane] = start
        state_ref[OWN:, lane] = start
        coef = scale * coef * jnp.where(mine, 1.0, 0.0)
        moments = moments + center * coef
        scaled_ref[:, lane] = coef.astype(bf16)
    shift = jnp.sum(moments, axis=1, keepdims=True)
    pltpu.make_async_copy(
        centers_ref.at[pl.ds(0, local_blocks)], local_rows, sem.at[7]
    ).wait()
    for r in range(local_blocks):
        local_ref[:, r * BLOCK : (r + 1) * BLOCK] = local_rows[r]
    for k, (target, turn, first, height) in enumerate(moves):
        pltpu.make_async_copy(
            source_ref.at[pl.ds(0, height), pl.ds(0, SHARE)], target, sem.at[2 + k]
        ).wait()

    def dot(turn, piece):
        return lax.dot_general(
            scaled_ref[:, turn * SHARE : (turn + 1) * SHARE],
            piece[...],
            LAST,
            preferred_element_type=f32,
        )

    far = jnp.concatenate([dot(2, far_a), dot(2, far_b)], axis=1)
    fit = (dot(0, own) + dot(1, right) + far + dot(3, left) - shift).astype(bf16)
    for x in range(4):
        fit_ref[x] = fit


def pick_blocks(blocks, dosage, centers, scales, warm):
    tall = jax.ShapeDtypeStruct((ROWS, SHARE), bf16)
    flat = jax.ShapeDtypeStruct((PART, SHARE), bf16)
    far = pl.BlockSpec(memory_space=pltpu.HBM)
    return pl.pallas_call(
        pick_kernel,
        in_specs=[pl.BlockSpec(memory_space=pltpu.SMEM), far, far, far, far],
        out_specs=[WHOLE] * 9,
        out_shape=[
            tall,
            tall,
            flat,
            flat,
            tall,
            jax.ShapeDtypeStruct((4, FITS, ROWS), bf16),
            jax.ShapeDtypeStruct((2, NS), f32),
            jax.ShapeDtypeStruct((1, dosage.shape[1]), f32),
            jax.ShapeDtypeStruct((2 * OWN, NS), f32),
        ],
        scratch_shapes=[
            pltpu.VMEM((SLOTS, 1, BLOCK), f32),
            pltpu.VMEM((SLOTS, 1, BLOCK), f32),
            pltpu.VMEM((dosage.shape[1] // BLOCK, 1, BLOCK), f32),
            pltpu.VMEM((FITS, NS), bf16),
            pltpu.VMEM((FITS, NS), f32),
            pltpu.SemaphoreType.DMA((9,)),
        ],
        name="pick_blocks",
    )(blocks, dosage, centers, scales, warm)


def send_gradient(residuals, wide_ref, pieces, extra_ref, out_ref):
    sums = sum(jnp.sum(part.astype(f32), axis=1, keepdims=True) for part in residuals)

    def half(residual, group):
        def dot(part, piece):
            return jnp.dot(part, piece[...], preferred_element_type=f32)

        tops = [dot(residual[:, :PART], piece) for piece in group[0::2]]
        bottoms = [dot(residual[:, PART:], piece) for piece in group[1::2]]
        return [top + bottom for top, bottom in zip(tops, bottoms)]

    both = zip(half(residuals[0], pieces[:8]), half(residuals[1], pieces[8:]))
    for j, (near, other) in enumerate(both):
        lane = pl.ds(j * SHARE, SHARE)
        piece = (near + other - wide_ref[1:2, lane] * sums).astype(bf16)
        for y in range(4):
            out_ref[y, :, lane] = piece
    if extra_ref is not None:
        for y in range(4):
            out_ref[y, :, NS:] = extra_ref[...]


def first_kernel(residual_ref, other_ref, wide_ref, *refs):
    send_gradient([residual_ref[...], other_ref[...]], wide_ref, refs[:16], None, refs[16])


def first_sweep(residual, other, wide, pieces):
    return pl.pallas_call(
        first_kernel,
        in_specs=[WHOLE] * 19,
        out_specs=WHOLE,
        out_shape=jax.ShapeDtypeStruct((4, OWN, NS), bf16),
        compiler_params=ROOM,
        name="first_sweep",
    )(residual, other, wide, *pieces)


def settle_kernel(
    local_blocks, penalty_ref, step_ref, arrived_ref, scales_ref, extra_ref, column_ref, rows, sem
):
    core = lax.axis_index("core")
    place = lax.axis_index("x")
    slot = lax.axis_index("z") * 4 + lax.axis_index("y")
    for i in range(MBLK):
        block = jnp.minimum(slot * MBLK + i, local_blocks - 1) + place * local_blocks
        pltpu.make_async_copy(scales_ref.at[block], rows.at[i], sem).start()
    first = arrived_ref[0].astype(f32)
    for source in range(1, PARTS):
        first = first + arrived_ref[source].astype(f32)
    edge = MBLK * HALF
    totals = first[edge : edge + 1] + first[edge + 1 : edge + 2]
    row = lax.broadcasted_iota(jnp.int32, (HALF, BLOCK), 0)
    lane = lax.broadcasted_iota(jnp.int32, (HALF, BLOCK), 1)
    counts = jnp.sum(jnp.where(lane == row % FOLDS, totals, 0.0), axis=1, keepdims=True)
    limit = jnp.zeros((HALF, BLOCK), f32)
    for q in range(HALF // FOLDS):
        limit = jnp.where(row // FOLDS == q, penalty_ref[core * (HALF // FOLDS) + q], limit)
    pltpu.make_async_copy(scales_ref.at[pl.ds(0, MBLK)], rows, sem).wait()
    few = lax.broadcasted_iota(jnp.int32, (OWN, BLOCK), 0)
    for i in range(MBLK):
        kkt = rows[i] * first[i * HALF : (i + 1) * HALF] / counts
        peak = jnp.max(jnp.abs(kkt) / limit, axis=0, keepdims=True)
        high = peak.astype(bf16).astype(f32)
        both = jnp.where(few == 0, high, jnp.where(few == 1, peak - high, 0.0))
        extra_ref[:, i * BLOCK : (i + 1) * BLOCK] = both.astype(bf16)
    step = jnp.zeros((OWN, BLOCK), f32)
    for j in range(OWN):
        step = jnp.where(few == j, step_ref[core * HALF + place * OWN + j], step)
    threshold = step * penalty_ref[core * (HALF // FOLDS) + place]
    few_lane = lane[:OWN]
    column_ref[...] = jnp.where(
        few_lane == 0, step, jnp.where(few_lane == 1, threshold, counts[:OWN])
    )


def settle(local_blocks, penalty, step_size, arrived, scales):
    small = pl.BlockSpec(memory_space=pltpu.SMEM)
    return pl.pallas_call(
        functools.partial(settle_kernel, local_blocks),
        in_specs=[small, small, WHOLE, pl.BlockSpec(memory_space=pltpu.HBM)],
        out_specs=[WHOLE] * 2,
        out_shape=[
            jax.ShapeDtypeStruct((OWN, PEAK), bf16),
            jax.ShapeDtypeStruct((OWN, BLOCK), f32),
        ],
        scratch_shapes=[pltpu.VMEM((MBLK, 1, BLOCK), f32), pltpu.SemaphoreType.DMA],
        compiler_params=ROOM,
        name="settle",
    )(penalty, step_size, arrived, scales)


def middle_kernel(got_ref, out_ref):
    total = got_ref[0, :, :NS].astype(f32)
    for y in range(1, 4):
        total = total + got_ref[y, :, :NS].astype(f32)
    total = total.astype(bf16)
    for z in range(8):
        out_ref[z, :, :NS] = total
        if got_ref.shape[2] > NS:
            for y in range(4):
                out_ref[z, :, NS + y * PEAK : NS + (y + 1) * PEAK] = got_ref[y, :, NS:]


def middle(got):
    width = NS + 4 * (got.shape[2] - NS)
    return pl.pallas_call(
        middle_kernel,
        in_specs=[WHOLE],
        out_specs=WHOLE,
        out_shape=jax.ShapeDtypeStruct((8, OWN, width), bf16),
        compiler_params=ROOM,
        name="middle",
    )(got)


def prox(got_ref, state_ref, wide_ref, column_ref, factor):
    total = got_ref[0, :, :NS].astype(f32)
    for z in range(1, 8):
        total = total + got_ref[z, :, :NS].astype(f32)
    step, threshold, counts = (column_ref[:, i : i + 1] for i in range(3))
    moved = state_ref[:OWN] + step * (wide_ref[0:1] * total / counts)
    current = moved - jnp.clip(moved, -threshold, threshold)
    return current + factor * (current - state_ref[OWN:]), current


def sweep_kernel(factor, has_extra, *refs):
    got_ref, state_ref, wide_ref, column_ref, samples_ref, other_ref = refs[:6]
    pieces = refs[6:22]
    extra_ref = refs[22] if has_extra else None
    out_ref, next_ref = refs[-2:]
    point, current = prox(got_ref, state_ref, wide_ref, column_ref, factor)
    next_ref[:OWN] = point
    next_ref[OWN:] = current
    weighted = wide_ref[0:1] * point
    shift = jnp.sum(wide_ref[1:2] * weighted, axis=1, keepdims=True)
    scaled = weighted.astype(bf16)

    def dot(turn, piece):
        return lax.dot_general(
            scaled[:, turn * SHARE : (turn + 1) * SHARE],
            piece[...],
            LAST,
            preferred_element_type=f32,
        )

    def half(ref, group):
        top = sum(dot(turn, piece) for turn, piece in enumerate(group[0::2]))
        bottom = sum(dot(turn, piece) for turn, piece in enumerate(group[1::2]))
        fitted = jnp.concatenate([top, bottom], axis=1) - shift
        fold = lax.broadcasted_iota(jnp.int32, (OWN, ROWS), 0).astype(f32)
        weight = jnp.where(ref[1:2] != fold, 1.0, 0.0)
        return (weight * (ref[0:1] - fitted)).astype(bf16)

    residuals = [half(samples_ref, pieces[:8]), half(other_ref, pieces[8:])]
    send_gradient(residuals, wide_ref, pieces, extra_ref, out_ref)


def sweep(factor, extra, *operands):
    width = NS if extra is None else NS + PEAK
    more = () if extra is None else (extra,)
    return pl.pallas_call(
        functools.partial(sweep_kernel, factor, extra is not None),
        in_specs=[WHOLE] * (len(operands) + len(more)),
        out_specs=[WHOLE] * 2,
        out_shape=[
            jax.ShapeDtypeStruct((4, OWN, width), bf16),
            jax.ShapeDtypeStruct((2 * OWN, NS), f32),
        ],
        compiler_params=ROOM,
        name="sweep",
    )(*operands, *more)


def last_kernel(got_ref, state_ref, wide_ref, column_ref, out_ref):
    current = prox(got_ref, state_ref, wide_ref, column_ref, 0.0)[1]
    for turn in range(4):
        piece = current[:, turn * SHARE : (turn + 1) * SHARE]
        spot = lax.rem(lax.axis_index("x") + turn, 4)
        out_ref[spot] = piece
        out_ref[spot + 4] = piece


def last(got, state, wide, columns):
    return pl.pallas_call(
        last_kernel,
        in_specs=[WHOLE] * 4,
        out_specs=WHOLE,
        out_shape=jax.ShapeDtypeStruct((8, OWN, SHARE), f32),
        compiler_params=ROOM,
        name="last",
    )(got, state, wide, columns)


def exchange(value, axis):
    return lax.all_to_all(value, axis, 0, 0, tiled=True)


def swap(value):
    return lax.ppermute(value, "core", [(0, 1), (1, 0)])


def onward(value):
    return lax.ppermute(value, "x", [(i, (i + 1) % 4) for i in range(4)])


def backward(value):
    return lax.ppermute(value, "x", [(i, (i + 3) % 4) for i in range(4)])


def turned(value, count, axis):
    twice = jnp.concatenate([value, value], axis=axis)
    return lax.dynamic_slice_in_dim(twice, count, value.shape[axis], axis)


def lanes(wide):
    return wide.reshape(wide.shape[0], -1, BLOCK).transpose(1, 0, 2)


def shards(
    dosage, centers, scales, phenotype, fold_ids, strong_blocks, warm_start, penalty, step_size
):
    rows, local_width = dosage.shape
    local_blocks = local_width // BLOCK
    core = lax.axis_index("core")
    place = lax.axis_index("x")
    first_fit = core * HALF + place * OWN
    other_fit = (1 - core) * HALF + place * OWN
    ahead = place * EACH

    warm = warm_start.T
    scale_rows = scales.reshape(-1, 1, BLOCK)
    own, right, far_a, far_b, left, fit_part, wide, local_centers, state = pick_blocks(
        strong_blocks, dosage, centers.reshape(-1, 1, BLOCK), scale_rows, warm
    )

    fit_part, phenotype, fold_ids = lax.optimization_barrier((fit_part, phenotype, fold_ids))
    samples = jnp.stack([phenotype, fold_ids.astype(f32)])
    samples_other = swap(samples)
    via_left = onward(far_a)
    via_right = backward(far_b)
    from_left = onward(right)
    from_right = backward(left)
    fitted = exchange(fit_part, "x")
    far_a = onward(via_left)
    far_b = backward(via_right)

    fit_folds = (jnp.arange(FITS, dtype=jnp.int32) % FOLDS).astype(f32)
    weights = (samples[1:] != fit_folds[:, None]).astype(f32)
    fitted = jnp.sum(fitted.astype(f32), axis=0)
    residual = (weights * (samples[:1] - fitted)).astype(bf16)
    column_sums = jnp.sum(residual.astype(f32), axis=1, keepdims=True)
    residual_own = lax.dynamic_slice_in_dim(residual, first_fit, OWN, 0)
    residual_other = swap(lax.dynamic_slice_in_dim(residual, other_fit, OWN, 0))

    cross = jnp.dot(residual, dosage, preferred_element_type=f32) - (
        local_centers * column_sums
    )
    keep = lax.dynamic_slice_in_dim(cross, core * HALF, HALF, 0)
    give = lax.dynamic_slice_in_dim(cross, (1 - core) * HALF, HALF, 0)
    summed = (keep + swap(give.astype(bf16)).astype(f32)).astype(bf16)
    padded = jnp.concatenate(
        [lanes(summed), jnp.zeros((PARTS * MBLK - local_blocks, HALF, BLOCK), bf16)], axis=0
    ).reshape(PARTS, MBLK * HALF, BLOCK)
    near = jnp.concatenate([samples, samples_other], axis=1)
    near_weights = (near[1:] != fit_folds[:FOLDS, None]).astype(f32)
    tally_rows = jnp.zeros((8, BLOCK), f32)
    tally_rows = tally_rows.at[0, :FOLDS].set(jnp.sum(near_weights[:, :rows], axis=1))
    tally_rows = tally_rows.at[1, :FOLDS].set(jnp.sum(near_weights[:, rows:], axis=1))
    message = jnp.concatenate(
        [padded, jnp.broadcast_to(tally_rows.astype(bf16)[None], (PARTS, 8, BLOCK))], axis=1
    )
    owner = jnp.repeat(turned(strong_blocks, ahead, 0)[:EACH] // local_blocks, BLOCK)[None, :]
    share = []
    for first, far in ((0, far_a), (PART, far_b)):
        piece = own[first : first + PART]
        for ahead, source in ((3, from_left), (1, from_right)):
            source = source[first : first + PART]
            piece = jnp.where(owner == (place + ahead) % 4, source, piece)
        share.append(jnp.where(owner == (place + 2) % 4, far, piece))
    arrived = exchange(message, PLANE)
    share_a, share_b, residual_other = lax.optimization_barrier((*share, residual_other))
    left_a = onward(share_a)
    right_b = backward(share_b)
    left_b = onward(share_b)
    right_a = backward(share_a)
    strong = [share_a, share_b, right_a, right_b, onward(left_a), backward(right_b), left_a, left_b]
    strong += [swap(piece) for piece in strong]
    strong = lax.optimization_barrier(tuple(strong))

    sent = first_sweep(residual_own, residual_other, wide, strong)
    sent, arrived = lax.optimization_barrier((sent, arrived))
    extra, columns = settle(local_blocks, penalty, step_size, arrived, scale_rows)

    got = exchange(middle(exchange(sent, "y")), "z")
    momentum = 1.0
    margin = None
    for round in range(1, ITERS):
        following = (1.0 + math.sqrt(1.0 + 4.0 * momentum * momentum)) / 2.0
        factor = (momentum - 1.0) / following
        sent, state = sweep(
            factor,
            extra if round == 1 else None,
            got,
            state,
            wide,
            columns,
            samples,
            samples_other,
            *strong,
        )
        got = exchange(middle(exchange(sent, "y")), "z")
        momentum = following
        if round == 1:
            peaks = got[:, :2, NS:].astype(f32)
            peaks = jnp.sum(peaks, axis=1).reshape(PARTS * PEAK)[:local_width]
            margin = jnp.maximum(peaks, swap(peaks))
    leaving = last(got, state, wide, columns)
    landed = exchange(leaving, ("core", "x"))
    return (margin, landed.reshape(FITS, SHARE).T)


def solution(mesh):
    cube = Mesh(mesh.devices.reshape(8, 4, 2, 4), ("z", "y", "core", "x"))
    samp = ("z", "y", "core")
    return jax.shard_map(
        shards,
        mesh=cube,
        in_specs=(P(samp, "x"), P(), P(), P(samp), P(samp), P(), P(), P(), P()),
        out_specs=(P("x"), P("x", None)),
        check_vma=False,
    )
```
